32 devices in a mesh: groups: 2 (over y), ctx: 8 (over z, x), mp: 2 (over core).
Axes of the slice: x: 2, y: 2, z: 4, core: 2. Of those that a mesh axis runs over, the one named last changes fastest.
Arguments:
- inputs: bfloat16 [2048, 2048], P(('groups', 'ctx'), 'mp'), parts along dimension 0, may hold values from -6 to 6
- cotangent: bfloat16 [2048, 2048], P(('groups', 'ctx'), 'mp'), parts along dimension 0, may hold values from -0.1875 to 0.1875
- filters: float32 [1024, 24], P('ctx'), may hold values from -0.1875 to 0.1875
- mixing: float32 [24, 2048], P(None, 'mp'), may hold values from -1.25 to 1.25
- ar_coef: float32 [3, 2048], P(None, 'mp'), may hold values from -3 to 3
Outputs:
- outputs: bfloat16 [2048, 2048], P(('groups', 'ctx'), 'mp'), parts along dimension 0
- grad_mixing: float32 [48, 2048], P('groups', 'mp'), parts along dimension 0
- grad_ar: float32 [6, 2048], P('groups', 'mp'), parts along dimension 0
The draws below stay inside these ranges and needn't reach their ends.
There are 2 independent parts, one for each index of `groups`. The reference program is written for one: setup_inputs(seed, part) draws one part's arguments, and reference() takes and returns one part's arrays. A program takes and returns all parts, laid end to end along the dimension named above; an argument that names none is the same for every part. Nothing has to cross between parts.
All inputs are finite; a program needn't handle non-finite values.
Results may differ from the reference program's by a relative error of at most 0.001.
Values may be sent and summed in bfloat16 or wider, within the bound.
No kernel may reach another device: no remote copies, remote signals or barrier semaphores. Data moves between devices by JAX's collectives and lax.ppermute only.
A program may use at most 64 MiB of HBM per device.

```python
import jax
import jax.numpy as jnp
from jax import lax

D = 2048
K = 24
ORDER = 3
SEQ = 1024


def levels(rng, extent, pieces, low, top_value):
    factor_of = 1.0
    for position, parts in pieces:
        draws = jax.random.uniform(jax.random.fold_in(jax.random.fold_in(rng, 6), position), (parts,), jnp.float32, low / len(pieces), top_value / len(pieces))
        factor_of = factor_of * jnp.repeat(jnp.exp(draws), extent[position] // parts).reshape((-1,) + (1,) * (len(extent) - 1 - position))
    return factor_of


def scatter_about(key, extent, deviation, bound, cuts=(), dtype=jnp.bfloat16):
    array = deviation * jax.random.normal(key, extent, jnp.float32)
    if cuts:
        array = array * levels(key, extent, cuts, -0.22, 0.18)
    return jnp.clip(array, -bound, bound).astype(dtype)


def setup_inputs(seed: int = 0, part: int = 0) -> dict:
    key_list = jax.random.split(jax.random.key(seed), 6)
    own_keys = jax.random.split(jax.random.fold_in(key_list[5], part), 6)
    return {
        "inputs": scatter_about(own_keys[0], (SEQ, D), 1.0, 6.0, ((0, 8), (1, 2))),
        "cotangent": scatter_about(own_keys[1], (SEQ, D), (SEQ ** -0.5), 0.1875, ((0, 8), (1, 2))),
        "filters": scatter_about(key_list[2], (SEQ, K), (SEQ ** -0.5), 0.1875, ((0, 8),), jnp.float32),
        "mixing": scatter_about(key_list[3], (K, D), K ** -0.5, 1.25, ((1, 2),), jnp.float32),
        "ar_coef": scatter_about(key_list[4], (ORDER, D), 0.5, 3.0, ((1, 2),), jnp.float32),
    }


def reference(inputs, cotangent, filters, mixing, ar_coef):
    total_len = 2 * SEQ
    signal = inputs.astype(jnp.float32)
    cot_rows = cotangent.astype(jnp.float32)
    kernel = jnp.dot(filters, mixing, precision=lax.Precision.HIGHEST)

    def per_block(blocks):
        sig_block, cot_block, ker_block = blocks
        sig_spec = jnp.fft.rfft(sig_block, n=total_len, axis=0)
        ker_spec = jnp.fft.rfft(ker_block, n=total_len, axis=0)
        cot_spec = jnp.fft.rfft(cot_block, n=total_len, axis=0)
        convolved = jnp.fft.irfft(sig_spec * ker_spec, n=total_len, axis=0)[:SEQ]
        lagged = jnp.fft.irfft(cot_spec * jnp.conj(sig_spec), n=total_len, axis=0)[:SEQ]
        return convolved.astype(jnp.float32), lagged.astype(jnp.float32)

    def split_cols(matrix):
        return matrix.reshape(SEQ, D // 128, 128).transpose(1, 0, 2)

    def join_cols(blocked):
        return blocked.transpose(1, 0, 2).reshape(SEQ, D)

    conv_blocks, lag_blocks = lax.map(per_block, (split_cols(signal), split_cols(cot_rows), split_cols(kernel)))
    convolved = join_cols(conv_blocks)
    lagged = join_cols(lag_blocks)
    padded = jnp.concatenate([jnp.zeros((ORDER, D), jnp.float32), signal], axis=0)
    autoreg = jnp.zeros((SEQ, D), jnp.float32)
    for lag_step in range(1, ORDER + 1):
        autoreg = autoreg + ar_coef[lag_step - 1] * padded[ORDER - lag_step:ORDER - lag_step + SEQ]
    outputs = (convolved + autoreg).astype(jnp.bfloat16)
    grad_mixing = jnp.dot(filters.T, lagged, precision=lax.Precision.HIGHEST)
    grad_ar = lagged[1:ORDER + 1]
    return outputs, grad_mixing, grad_ar
```

```python
import functools
import math

import jax
import jax.numpy as jnp
import numpy as np
from jax import lax
from jax.experimental import pallas as pl
from jax.experimental.pallas import tpu as pltpu
from jax.sharding import PartitionSpec as P

ORDER = 3
LANES = 128
ROWS = 16

f32 = jnp.float32
bf16 = jnp.bfloat16
highest = lax.Precision.HIGHEST


def phase_tables(seq_len):
    radix_len = math.gcd(seq_len, 128)
    outer_len = 2 * seq_len // radix_len
    half_outer = outer_len // 2
    total_len = 2 * seq_len
    low_index = jnp.arange(half_outer, dtype=jnp.int32)
    outer_index = jnp.arange(outer_len, dtype=jnp.int32)
    radix_index = jnp.arange(radix_len, dtype=jnp.int32)
    outer_angle = (low_index[:, None] * outer_index[None, :] % outer_len).astype(jnp.float32) * (
        2.0 * math.pi / outer_len
    )
    twist_angle = (outer_index[:, None] * radix_index[None, :] % total_len).astype(jnp.float32) * (
        2.0 * math.pi / total_len
    )
    radix_angle = (radix_index[:, None] * radix_index[None, :] % radix_len).astype(jnp.float32) * (
        2.0 * math.pi / radix_len
    )
    return (
        jnp.cos(outer_angle),
        jnp.sin(outer_angle),
        jnp.cos(twist_angle),
        jnp.sin(twist_angle),
        jnp.cos(radix_angle),
        jnp.sin(radix_angle),
    )


def forward_spectrum(signal, tables):
    outer_cos, outer_sin, twist_cos, twist_sin, radix_cos, radix_sin = tables
    channels = signal.shape[0]
    folded = signal.reshape(channels, outer_cos.shape[0], radix_cos.shape[0])
    first_real = jnp.einsum("chr,hk->ckr", folded, outer_cos, precision=highest)
    first_imag = -jnp.einsum("chr,hk->ckr", folded, outer_sin, precision=highest)
    turned_real = first_real * twist_cos + first_imag * twist_sin
    turned_imag = first_imag * twist_cos - first_real * twist_sin
    spec_real = jnp.einsum("ckr,rq->ckq", turned_real, radix_cos, precision=highest) + jnp.einsum(
        "ckr,rq->ckq", turned_imag, radix_sin, precision=highest
    )
    spec_imag = jnp.einsum("ckr,rq->ckq", turned_imag, radix_cos, precision=highest) - jnp.einsum(
        "ckr,rq->ckq", turned_real, radix_sin, precision=highest
    )
    return (spec_real, spec_imag)


def inverse_spectrum(spec_real, spec_imag, tables):
    outer_cos, outer_sin, twist_cos, twist_sin, radix_cos, radix_sin = tables
    back_real = jnp.einsum("ckq,rq->ckr", spec_real, radix_cos, precision=highest) - jnp.einsum(
        "ckq,rq->ckr", spec_imag, radix_sin, precision=highest
    )
    back_imag = jnp.einsum("ckq,rq->ckr", spec_real, radix_sin, precision=highest) + jnp.einsum(
        "ckq,rq->ckr", spec_imag, radix_cos, precision=highest
    )
    untwist_real = back_real * twist_cos - back_imag * twist_sin
    untwist_imag = back_real * twist_sin + back_imag * twist_cos
    folded = jnp.einsum("ckr,hk->chr", untwist_real, outer_cos, precision=highest) - jnp.einsum(
        "ckr,hk->chr", untwist_imag, outer_sin, precision=highest
    )
    channels = folded.shape[0]
    total_len = 2 * folded.shape[1] * folded.shape[2]
    return folded.reshape(channels, -1) / total_len


def local_general(inputs, cotangent, filters, mixing, ar_coef):
    tok_rows, local_width = inputs.shape
    ctx_count = lax.axis_size("ctx")
    ctx_place = lax.axis_index("ctx")
    narrow = local_width // ctx_count
    seq_len = tok_rows * ctx_count
    tables = phase_tables(seq_len)
    seq_cols = lax.all_to_all(inputs.T, "ctx", split_axis=0, concat_axis=1, tiled=True)
    signal = seq_cols.astype(jnp.float32)
    filter_all = lax.all_gather(filters, "ctx", axis=0, tiled=True)
    mix_local = lax.dynamic_slice_in_dim(mixing, ctx_place * narrow, narrow, 1)
    kernel = jnp.einsum("lk,kc->cl", filter_all, mix_local, precision=highest)
    sig_real, sig_imag = forward_spectrum(signal, tables)
    ker_real, ker_imag = forward_spectrum(kernel, tables)
    convolved = inverse_spectrum(
        ker_real * sig_real - ker_imag * sig_imag, ker_real * sig_imag + ker_imag * sig_real, tables
    )
    cot_cols = lax.all_to_all(cotangent.T, "ctx", split_axis=0, concat_axis=1, tiled=True)
    cot_real, cot_imag = forward_spectrum(cot_cols.astype(jnp.float32), tables)
    lagged = inverse_spectrum(
        cot_real * sig_real + cot_imag * sig_imag, cot_imag * sig_real - cot_real * sig_imag, tables
    )
    ar_local = lax.dynamic_slice_in_dim(ar_coef, ctx_place * narrow, narrow, 1)
    padded = jnp.pad(signal, ((0, 0), (ORDER, 0)))
    autoreg = jnp.zeros_like(signal)
    for lag_step in range(1, ORDER + 1):
        autoreg = (
            autoreg
            + ar_local[lag_step - 1][:, None]
            * padded[:, ORDER - lag_step : ORDER - lag_step + seq_len]
        )
    out_cols = (convolved + autoreg).astype(jnp.bfloat16)
    outputs = lax.all_to_all(out_cols, "ctx", split_axis=1, concat_axis=0, tiled=True).T
    mix_piece = jnp.einsum("lk,cl->kc", filter_all, lagged, precision=highest)
    grad_mixing, grad_ar = (
        lax.all_gather(mix_piece, "ctx", axis=1, tiled=True),
        lax.all_gather(lagged[:, 1 : ORDER + 1].T, "ctx", axis=1, tiled=True),
    )
    return (outputs, grad_mixing, grad_ar)


def split_pair(value):
    high = value.astype(bf16)
    return high, (value - high.astype(f32)).astype(bf16)


def turn(count, k):
    angle = math.pi * (k + 0.5) / count
    return math.cos(angle), math.sin(angle)


def half_forward(xs):
    n = len(xs)
    if n == 1:
        return [(xs[0], None)]
    even, odd = half_forward(xs[0::2]), half_forward(xs[1::2])
    low, high = [], []
    for k in range(n // 2):
        c, s = turn(n, k)
        er, ei = even[k]
        orr, oi = odd[k]
        if oi is None:
            tr, ti = orr * c, orr * (-s)
            low.append((er + tr, ti))
            high.append((er - tr, ti))
        else:
            tr, ti = orr * c + oi * s, oi * c - orr * s
            low.append((er + tr, ei + ti))
            high.append((er - tr, ti - ei))
    return low + high[::-1]


def half_inverse(us):
    n = len(us)
    if n == 1:
        return [us[0][0]]
    even, odd = [], []
    for k in range(n // 2):
        c, s = turn(n, k)
        (ar, ai), (br, bi) = us[k], us[n - 1 - k]
        dr, di = ar - br, ai + bi
        if n == 2:
            even.append((ar + br, None))
            odd.append((dr * c - di * s, None))
        else:
            even.append((ar + br, ai - bi))
            odd.append((dr * c - di * s, dr * s + di * c))
    out = [None] * n
    out[0::2] = half_inverse(even)
    out[1::2] = half_inverse(odd)
    return out


def dft_constants(half, radix):
    index = np.arange(radix)
    angle = 2.0 * np.pi * (index[:, None] * index[None, :] % radix) / radix
    c, s = np.cos(angle), np.sin(angle)
    forward = np.block([[c, s], [-s, c]])

    def stacked(matrix):
        matrix = matrix.astype(np.float32)
        high = matrix.astype(jnp.bfloat16)
        low = (matrix - high.astype(np.float32)).astype(jnp.bfloat16)
        return np.concatenate([high, low], axis=0)

    theta = 2.0 * np.pi * index[:, None] * (np.arange(half)[None, :] + 0.5) / (2 * half * radix)
    twist = np.concatenate([np.cos(theta), np.sin(theta)], axis=1).astype(np.float32)
    return stacked(forward), stacked(forward.T), twist, np.ascontiguousarray(twist.T)


def dot(a, b):
    return jnp.dot(a, b, preferred_element_type=f32)


def outer_forward(src_ref, tw_ref, high_ref, low_ref, half, radix):
    for r in range(0, radix, ROWS):
        parts = half_forward([src_ref[h, r : r + ROWS, :].astype(f32) for h in range(half)])
        for k, (re, im) in enumerate(parts):
            c, s = tw_ref[r : r + ROWS, k : k + 1], tw_ref[r : r + ROWS, half + k : half + k + 1]
            lanes = slice(k * LANES, (k + 1) * LANES)
            for base, value in ((0, re * c + im * s), (radix, im * c - re * s)):
                high, low = split_pair(value)
                high_ref[base + r : base + r + ROWS, lanes] = high
                low_ref[base + r : base + r + ROWS, lanes] = low


def inner_dft(w_ref, high_ref, low_ref, lanes):
    both = w_ref.shape[0] // 2
    first = dot(w_ref[...], high_ref[:, lanes])
    return first[:both] + first[both:] + dot(w_ref[:both, :], low_ref[:, lanes])


def pack_kernel(x_ref, g_ref, f_ref, first_ref, second_ref, *, count):
    tok = x_ref.shape[0]
    high, low = split_pair(f_ref[...].T)
    taps = high.shape[0]
    pieces = jnp.concatenate([high.astype(f32), low.astype(f32)], axis=0).astype(bf16)
    for j in range(count):
        lanes = slice(j * LANES, (j + 1) * LANES)
        first_ref[j, 0:tok, :] = x_ref[:, lanes]
        first_ref[j, tok : tok + 2 * taps, :] = pieces
        second_ref[j] = g_ref[:, lanes]


def conv_kernel(
    place_ref,
    recv_ref,
    mix_ref,
    ar_ref,
    wf_ref,
    wi_ref,
    tw_ref,
    twt_ref,
    y_ref,
    spec_ref,
    taps_ref,
    a_high,
    a_low,
    b_high,
    b_low,
    *,
    half,
    radix,
    kp,
):
    taps = mix_ref.shape[0]
    order = ar_ref.shape[0]
    width = 2 * radix
    blocks = []
    for h in range(half):
        both = recv_ref[h, radix : radix + 2 * taps, :].astype(f32)
        value = both[:taps] + both[taps:]
        extra = jnp.zeros((kp - taps, radix), f32)
        if h == 0:
            row = lax.broadcasted_iota(jnp.int32, extra.shape, 0)
            lane = lax.broadcasted_iota(jnp.int32, extra.shape, 1)
            extra = jnp.where((row < order) & (lane == row + 1), 1.0, extra)
        blocks.append(jnp.concatenate([value, extra], axis=0))
    for k, (re, im) in enumerate(half_forward(blocks)):
        c, s = twt_ref[k : k + 1, :], twt_ref[half + k : half + k + 1, :]
        value = jnp.concatenate([re * c + im * s, im * c - re * s], axis=1)
        high, low = split_pair(value)
        a_high[k * kp : (k + 1) * kp, 0:width] = high
        a_low[k * kp : (k + 1) * kp, 0:width] = low
    n_rows = half * kp
    filt = (
        dot(a_high[0:n_rows, 0:width], wi_ref[0:width, :])
        + dot(a_low[0:n_rows, 0:width], wi_ref[0:width, :])
        + dot(a_high[0:n_rows, 0:width], wi_ref[width : 2 * width, :])
    )
    f_high, f_low = split_pair(filt)
    for k in range(half):
        rows = slice(k * kp, (k + 1) * kp)
        lanes = slice(k * width, (k + 1) * width)
        taps_ref[0:kp, lanes] = f_high[rows]
        taps_ref[kp : 2 * kp, lanes] = f_low[rows]
    weights = jnp.concatenate(
        [mix_ref[...], ar_ref[...], jnp.zeros((kp - taps - order, LANES), f32)], axis=0
    ) * (1.0 / (half * radix))
    m_high, m_low = split_pair(weights)
    zero = jnp.zeros_like(m_high)

    def diagonal(m):
        return jnp.concatenate(
            [jnp.concatenate([m, zero], axis=1), jnp.concatenate([zero, m], axis=1)], axis=0
        )

    d_high, d_low = diagonal(m_high), diagonal(m_low)
    mixer = jnp.concatenate([d_high, d_high, d_low], axis=0)

    outer_forward(recv_ref, tw_ref, b_high, b_low, half, radix)
    for m in range(half // 2):
        lanes = slice(m * 2 * LANES, (m + 1) * 2 * LANES)
        rows = slice(2 * m * kp, 2 * (m + 1) * kp)
        spec = inner_dft(wf_ref, b_high, b_low, lanes)
        spec_ref[:, lanes] = spec
        ker = lax.dot_general(
            jnp.concatenate([f_high[rows], f_low[rows], f_high[rows]], axis=0),
            mixer,
            (((0,), (0,)), ((), ())),
            preferred_element_type=f32,
        )
        sr, si, kr, ki = spec[:radix], spec[radix:], ker[:radix], ker[radix:]
        for base, value in ((0, sr * kr - si * ki), (radix, sr * ki + si * kr)):
            high, low = split_pair(value)
            a_high[base : base + radix, lanes] = high
            a_low[base : base + radix, lanes] = low
    backs = []
    for m in range(half // 2):
        lanes = slice(m * 2 * LANES, (m + 1) * 2 * LANES)
        backs.append(inner_dft(wi_ref, a_high, a_low, lanes))
    for r in range(0, radix, ROWS):
        us = []
        for k in range(half):
            lanes = slice((k % 2) * LANES, (k % 2 + 1) * LANES)
            gr = backs[k // 2][r : r + ROWS, lanes]
            gi = backs[k // 2][radix + r : radix + r + ROWS, lanes]
            c, s = tw_ref[r : r + ROWS, k : k + 1], tw_ref[r : r + ROWS, half + k : half + k + 1]
            us.append((gr * c - gi * s, gr * s + gi * c))
        for h, value in enumerate(half_inverse(us)):
            y_ref[h, r : r + ROWS, :] = value.astype(bf16)


def grad_kernel(recv_ref, spec_ref, taps_ref, wf_ref, tw_ref, out_ref, b_high, b_low, p_high, p_low, *, half, radix, kp):
    outer_forward(recv_ref, tw_ref, b_high, b_low, half, radix)
    for m in range(half // 2):
        lanes = slice(m * 2 * LANES, (m + 1) * 2 * LANES)
        cot = inner_dft(wf_ref, b_high, b_low, lanes)
        spec = spec_ref[:, lanes]
        cr, ci, sr, si = cot[:radix], cot[radix:], spec[:radix], spec[radix:]
        for base, value in ((0, cr * sr + ci * si), (radix, ci * sr - cr * si)):
            high, low = split_pair(value)
            for side in range(2):
                row = (2 * m + side) * 2 * radix + base
                part = slice(side * LANES, (side + 1) * LANES)
                p_high[row : row + radix, :] = high[:, part]
                p_low[row : row + radix, :] = low[:, part]
    first = dot(taps_ref[...], p_high[...])
    grads = (first[:kp] + first[kp:] + dot(taps_ref[0:kp, :], p_low[...])) * (1.0 / (half * radix))
    for j in range(out_ref.shape[0]):
        out_ref[j] = grads


def unpack_kernel(y_ref, g_ref, out_ref, mix_ref, ar_ref, *, count):
    taps, order = mix_ref.shape[0], ar_ref.shape[0]
    for j in range(count):
        lanes = slice(j * LANES, (j + 1) * LANES)
        out_ref[:, lanes] = y_ref[j]
        mix_ref[:, lanes] = g_ref[j, 0:taps, :]
        ar_ref[:, lanes] = g_ref[j, taps : taps + order, :]


def shape_of(*dims, dtype=f32):
    return jax.ShapeDtypeStruct(dims, dtype)


def local_tiled(inputs, cotangent, filters, mixing, ar_coef):
    tok_rows, local_width = inputs.shape
    count = lax.axis_size("ctx")
    taps, order = filters.shape[1], ar_coef.shape[0]
    half, radix = count, tok_rows
    kp = -(-(taps + order) // 8) * 8
    wf, wi, twist, twist_t = dft_constants(half, radix)
    rows = tok_rows + 2 * taps

    first, second = pl.pallas_call(
        functools.partial(pack_kernel, count=count),
        out_shape=(
            shape_of(count, rows, LANES, dtype=bf16),
            shape_of(count, tok_rows, LANES, dtype=bf16),
        ),
        name="pack",
    )(inputs, cotangent, filters)
    swap = functools.partial(lax.all_to_all, axis_name="ctx", split_axis=0, concat_axis=0, tiled=True)
    first = swap(first)
    second = swap(second)

    whole = lambda *dims: pl.BlockSpec(dims, lambda i, place: (0,) * len(dims))
    place = lax.axis_index("ctx").astype(jnp.int32).reshape(1)
    span = half * LANES
    y_cols, spec, spectra = pl.pallas_call(
        functools.partial(conv_kernel, half=half, radix=radix, kp=kp),
        out_shape=(
            shape_of(count, tok_rows, LANES, dtype=bf16),
            shape_of(2 * radix, span),
            shape_of(2 * kp, half * 2 * radix, dtype=bf16),
        ),
        grid_spec=pltpu.PrefetchScalarGridSpec(
            num_scalar_prefetch=1,
            grid=(1,),
            in_specs=[
                whole(count, rows, LANES),
                pl.BlockSpec((taps, LANES), lambda i, place: (0, place[0])),
                pl.BlockSpec((order, LANES), lambda i, place: (0, place[0])),
                whole(*wf.shape),
                whole(*wi.shape),
                whole(*twist.shape),
                whole(*twist_t.shape),
            ],
            out_specs=(
                whole(count, tok_rows, LANES),
                whole(2 * radix, span),
                whole(2 * kp, half * 2 * radix),
            ),
            scratch_shapes=[pltpu.VMEM((2 * radix, span), bf16)] * 4,
        ),
        cost_estimate=pl.CostEstimate(flops=3_000_000_000, bytes_accessed=3_000_000, transcendentals=0),
        name="conv",
    )(place, first, mixing, ar_coef, wf, wi, twist, twist_t)
    y_rows = swap(y_cols)

    grads = pl.pallas_call(
        functools.partial(grad_kernel, half=half, radix=radix, kp=kp),
        out_shape=shape_of(count, kp, LANES),
        scratch_shapes=[pltpu.VMEM((2 * radix, span), bf16)] * 2
        + [pltpu.VMEM((half * 2 * radix, LANES), bf16)] * 2,
        cost_estimate=pl.CostEstimate(flops=1_500_000_000, bytes_accessed=3_000_000, transcendentals=0),
        name="grads",
    )(second, spec, spectra, wf, twist)
    grads = swap(grads)

    return pl.pallas_call(
        functools.partial(unpack_kernel, count=count),
        out_shape=(
            shape_of(tok_rows, local_width, dtype=bf16),
            shape_of(taps, local_width),
            shape_of(order, local_width),
        ),
        name="unpack",
    )(y_rows, grads)


def local(inputs, cotangent, filters, mixing, ar_coef):
    tok_rows, local_width = inputs.shape
    count = lax.axis_size("ctx")
    tiled = (
        local_width == count * LANES
        and tok_rows == LANES
        and count in (2, 4, 8, 16)
        and filters.shape[1] % 8 == 0
    )
    return (local_tiled if tiled else local_general)(inputs, cotangent, filters, mixing, ar_coef)


def solution(mesh):
    return jax.shard_map(
        local,
        mesh=mesh,
        in_specs=(
            P(("groups", "ctx"), "mp"),
            P(("groups", "ctx"), "mp"),
            P("ctx", None),
            P(None, "mp"),
            P(None, "mp"),
        ),
        out_specs=(P(("groups", "ctx"), "mp"), P("groups", "mp"), P("groups", "mp")),
        check_vma=False,
    )
```

```python
import functools
import math

import jax
import jax.numpy as jnp
import numpy as np
from jax import lax
from jax.experimental import pallas as pl
from jax.experimental.pallas import tpu as pltpu
from jax.sharding import PartitionSpec as P

ORDER = 3
LANES = 128
ROWS = 16

f32 = jnp.float32
bf16 = jnp.bfloat16
highest = lax.Precision.HIGHEST


def phase_tables(seq_len):
    radix_len = math.gcd(seq_len, 128)
    outer_len = 2 * seq_len // radix_len
    half_outer = outer_len // 2
    total_len = 2 * seq_len
    low_index = jnp.arange(half_outer, dtype=jnp.int32)
    outer_index = jnp.arange(outer_len, dtype=jnp.int32)
    radix_index = jnp.arange(radix_len, dtype=jnp.int32)
    outer_angle = (low_index[:, None] * outer_index[None, :] % outer_len).astype(jnp.float32) * (
        2.0 * math.pi / outer_len
    )
    twist_angle = (outer_index[:, None] * radix_index[None, :] % total_len).astype(jnp.float32) * (
        2.0 * math.pi / total_len
    )
    radix_angle = (radix_index[:, None] * radix_index[None, :] % radix_len).astype(jnp.float32) * (
        2.0 * math.pi / radix_len
    )
    return (
        jnp.cos(outer_angle),
        jnp.sin(outer_angle),
        jnp.cos(twist_angle),
        jnp.sin(twist_angle),
        jnp.cos(radix_angle),
        jnp.sin(radix_angle),
    )


def forward_spectrum(signal, tables):
    outer_cos, outer_sin, twist_cos, twist_sin, radix_cos, radix_sin = tables
    channels = signal.shape[0]
    folded = signal.reshape(channels, outer_cos.shape[0], radix_cos.shape[0])
    first_real = jnp.einsum("chr,hk->ckr", folded, outer_cos, precision=highest)
    first_imag = -jnp.einsum("chr,hk->ckr", folded, outer_sin, precision=highest)
    turned_real = first_real * twist_cos + first_imag * twist_sin
    turned_imag = first_imag * twist_cos - first_real * twist_sin
    spec_real = jnp.einsum("ckr,rq->ckq", turned_real, radix_cos, precision=highest) + jnp.einsum(
        "ckr,rq->ckq", turned_imag, radix_sin, precision=highest
    )
    spec_imag = jnp.einsum("ckr,rq->ckq", turned_imag, radix_cos, precision=highest) - jnp.einsum(
        "ckr,rq->ckq", turned_real, radix_sin, precision=highest
    )
    return (spec_real, spec_imag)


def inverse_spectrum(spec_real, spec_imag, tables):
    outer_cos, outer_sin, twist_cos, twist_sin, radix_cos, radix_sin = tables
    back_real = jnp.einsum("ckq,rq->ckr", spec_real, radix_cos, precision=highest) - jnp.einsum(
        "ckq,rq->ckr", spec_imag, radix_sin, precision=highest
    )
    back_imag = jnp.einsum("ckq,rq->ckr", spec_real, radix_sin, precision=highest) + jnp.einsum(
        "ckq,rq->ckr", spec_imag, radix_cos, precision=highest
    )
    untwist_real = back_real * twist_cos - back_imag * twist_sin
    untwist_imag = back_real * twist_sin + back_imag * twist_cos
    folded = jnp.einsum("ckr,hk->chr", untwist_real, outer_cos, precision=highest) - jnp.einsum(
        "ckr,hk->chr", untwist_imag, outer_sin, precision=highest
    )
    channels = folded.shape[0]
    total_len = 2 * folded.shape[1] * folded.shape[2]
    return folded.reshape(channels, -1) / total_len


def local_general(inputs, cotangent, filters, mixing, ar_coef):
    tok_rows, local_width = inputs.shape
    ctx_count = lax.axis_size("ctx")
    ctx_place = lax.axis_index("ctx")
    narrow = local_width // ctx_count
    seq_len = tok_rows * ctx_count
    tables = phase_tables(seq_len)
    seq_cols = lax.all_to_all(inputs.T, "ctx", split_axis=0, concat_axis=1, tiled=True)
    signal = seq_cols.astype(jnp.float32)
    filter_all = lax.all_gather(filters, "ctx", axis=0, tiled=True)
    mix_local = lax.dynamic_slice_in_dim(mixing, ctx_place * narrow, narrow, 1)
    kernel = jnp.einsum("lk,kc->cl", filter_all, mix_local, precision=highest)
    sig_real, sig_imag = forward_spectrum(signal, tables)
    ker_real, ker_imag = forward_spectrum(kernel, tables)
    convolved = inverse_spectrum(
        ker_real * sig_real - ker_imag * sig_imag, ker_real * sig_imag + ker_imag * sig_real, tables
    )
    cot_cols = lax.all_to_all(cotangent.T, "ctx", split_axis=0, concat_axis=1, tiled=True)
    cot_real, cot_imag = forward_spectrum(cot_cols.astype(jnp.float32), tables)
    lagged = inverse_spectrum(
        cot_real * sig_real + cot_imag * sig_imag, cot_imag * sig_real - cot_real * sig_imag, tables
    )
    ar_local = lax.dynamic_slice_in_dim(ar_coef, ctx_place * narrow, narrow, 1)
    padded = jnp.pad(signal, ((0, 0), (ORDER, 0)))
    autoreg = jnp.zeros_like(signal)
    for lag_step in range(1, ORDER + 1):
        autoreg = (
            autoreg
            + ar_local[lag_step - 1][:, None]
            * padded[:, ORDER - lag_step : ORDER - lag_step + seq_len]
        )
    out_cols = (convolved + autoreg).astype(jnp.bfloat16)
    outputs = lax.all_to_all(out_cols, "ctx", split_axis=1, concat_axis=0, tiled=True).T
    mix_piece = jnp.einsum("lk,cl->kc", filter_all, lagged, precision=highest)
    grad_mixing, grad_ar = (
        lax.all_gather(mix_piece, "ctx", axis=1, tiled=True),
        lax.all_gather(lagged[:, 1 : ORDER + 1].T, "ctx", axis=1, tiled=True),
    )
    return (outputs, grad_mixing, grad_ar)


def split_pair(value):
    high = value.astype(bf16)
    return high, (value - high.astype(f32)).astype(bf16)


def turn(count, k):
    angle = math.pi * (k + 0.5) / count
    return math.cos(angle), math.sin(angle)


def half_forward(xs):
    n = len(xs)
    if n == 1:
        return [(xs[0], None)]
    even, odd = half_forward(xs[0::2]), half_forward(xs[1::2])
    low, high = [], []
    for k in range(n // 2):
        c, s = turn(n, k)
        er, ei = even[k]
        orr, oi = odd[k]
        if oi is None:
            tr, ti = orr * c, orr * (-s)
            low.append((er + tr, ti))
            high.append((er - tr, ti))
        else:
            tr, ti = orr * c + oi * s, oi * c - orr * s
            low.append((er + tr, ei + ti))
            high.append((er - tr, ti - ei))
    return low + high[::-1]


def half_inverse(us):
    n = len(us)
    if n == 1:
        return [us[0][0]]
    even, odd = [], []
    for k in range(n // 2):
        c, s = turn(n, k)
        (ar, ai), (br, bi) = us[k], us[n - 1 - k]
        dr, di = ar - br, ai + bi
        if n == 2:
            even.append((ar + br, None))
            odd.append((dr * c - di * s, None))
        else:
            even.append((ar + br, ai - bi))
            odd.append((dr * c - di * s, dr * s + di * c))
    out = [None] * n
    out[0::2] = half_inverse(even)
    out[1::2] = half_inverse(odd)
    return out


def dft_constants(half, radix):
    index = np.arange(radix)
    angle = 2.0 * np.pi * (index[:, None] * index[None, :] % radix) / radix
    c, s = np.cos(angle), np.sin(angle)
    forward = np.block([[c, s], [-s, c]])

    def stacked(matrix):
        matrix = matrix.astype(np.float32)
        high = matrix.astype(jnp.bfloat16)
        low = (matrix - high.astype(np.float32)).astype(jnp.bfloat16)
        return np.concatenate([high, low], axis=0)

    theta = 2.0 * np.pi * index[:, None] * (np.arange(half)[None, :] + 0.5) / (2 * half * radix)
    twist = np.concatenate([np.cos(theta), np.sin(theta)], axis=1).astype(np.float32)
    return stacked(forward), stacked(forward.T), twist, np.ascontiguousarray(twist.T)


def dot(a, b):
    return jnp.dot(a, b, preferred_element_type=f32)


def outer_forward(src_ref, start, tw_ref, high_ref, low_ref, half, radix):
    for r in range(0, radix, ROWS):
        parts = half_forward([src_ref[h, start + r : start + r + ROWS, :].astype(f32) for h in range(half)])
        for k, (re, im) in enumerate(parts):
            c, s = tw_ref[r : r + ROWS, k : k + 1], tw_ref[r : r + ROWS, half + k : half + k + 1]
            lanes = slice(k * LANES, (k + 1) * LANES)
            for base, value in ((0, re * c + im * s), (radix, im * c - re * s)):
                high, low = split_pair(value)
                high_ref[base + r : base + r + ROWS, lanes] = high
                low_ref[base + r : base + r + ROWS, lanes] = low


def inner_dft(w_ref, high_ref, low_ref, lanes):
    both = w_ref.shape[0] // 2
    first = dot(w_ref[...], high_ref[:, lanes])
    return first[:both] + first[both:] + dot(w_ref[:both, :], low_ref[:, lanes])


def pack_kernel(x_ref, g_ref, f_ref, send_ref):
    tok = x_ref.shape[0]
    high, low = split_pair(f_ref[...])
    taps = high.shape[0]
    pieces = jnp.concatenate([high.astype(f32), low.astype(f32)], axis=0).astype(bf16)
    for j in range(send_ref.shape[0]):
        lanes = slice(j * LANES, (j + 1) * LANES)
        send_ref[j, 0:tok, :] = x_ref[:, lanes]
        send_ref[j, tok : 2 * tok, :] = g_ref[:, lanes]
        send_ref[j, 2 * tok : 2 * tok + 2 * taps, :] = pieces


def main_kernel(
    place_ref,
    recv_ref,
    mix_ref,
    ar_ref,
    wf_ref,
    wi_ref,
    tw_ref,
    twt_ref,
    out_ref,
    a_high,
    a_low,
    b_high,
    b_low,
    spec_ref,
    taps_ref,
    p_high,
    p_low,
    *,
    half,
    radix,
    kp,
):
    taps = mix_ref.shape[0]
    order = ar_ref.shape[0]
    width = 2 * radix
    scale = 1.0 / (half * radix)
    blocks = []
    for h in range(half):
        both = recv_ref[h, 2 * radix : 2 * radix + 2 * taps, :].astype(f32)
        value = both[:taps] + both[taps:]
        extra = jnp.zeros((kp - taps, radix), f32)
        if h == 0:
            row = lax.broadcasted_iota(jnp.int32, extra.shape, 0)
            lane = lax.broadcasted_iota(jnp.int32, extra.shape, 1)
            extra = jnp.where((row < order) & (lane == row + 1), 1.0, extra)
        blocks.append(jnp.concatenate([value, extra], axis=0))
    for k, (re, im) in enumerate(half_forward(blocks)):
        c, s = twt_ref[k : k + 1, :], twt_ref[half + k : half + k + 1, :]
        value = jnp.concatenate([re * c + im * s, im * c - re * s], axis=1)
        high, low = split_pair(value)
        a_high[k * kp : (k + 1) * kp, 0:width] = high
        a_low[k * kp : (k + 1) * kp, 0:width] = low
    n_rows = half * kp
    filt = (
        dot(a_high[0:n_rows, 0:width], wi_ref[0:width, :])
        + dot(a_low[0:n_rows, 0:width], wi_ref[0:width, :])
        + dot(a_high[0:n_rows, 0:width], wi_ref[width : 2 * width, :])
    )
    f_high, f_low = split_pair(filt)
    for k in range(half):
        rows = slice(k * kp, (k + 1) * kp)
        lanes = slice(k * width, (k + 1) * width)
        taps_ref[0:kp, lanes] = f_high[rows]
        taps_ref[kp : 2 * kp, lanes] = f_low[rows]
    weights = (
        jnp.concatenate([mix_ref[...], ar_ref[...], jnp.zeros((kp - taps - order, LANES), f32)], axis=0)
        * scale
    )
    m_high, m_low = split_pair(weights)
    zero = jnp.zeros_like(m_high)

    def diagonal(m):
        return jnp.concatenate(
            [jnp.concatenate([m, zero], axis=1), jnp.concatenate([zero, m], axis=1)], axis=0
        )

    d_high, d_low = diagonal(m_high), diagonal(m_low)
    mixer = jnp.concatenate([d_high, d_high, d_low], axis=0)

    outer_forward(recv_ref, 0, tw_ref, b_high, b_low, half, radix)
    for m in range(half // 2):
        lanes = slice(m * 2 * LANES, (m + 1) * 2 * LANES)
        rows = slice(2 * m * kp, 2 * (m + 1) * kp)
        spec = inner_dft(wf_ref, b_high, b_low, lanes)
        spec_ref[:, lanes] = spec
        ker = lax.dot_general(
            jnp.concatenate([f_high[rows], f_low[rows], f_high[rows]], axis=0),
            mixer,
            (((0,), (0,)), ((), ())),
            preferred_element_type=f32,
        )
        sr, si, kr, ki = spec[:radix], spec[radix:], ker[:radix], ker[radix:]
        for base, value in ((0, sr * kr - si * ki), (radix, sr * ki + si * kr)):
            high, low = split_pair(value)
            a_high[base : base + radix, lanes] = high
            a_low[base : base + radix, lanes] = low
    backs = []
    for m in range(half // 2):
        lanes = slice(m * 2 * LANES, (m + 1) * 2 * LANES)
        backs.append(inner_dft(wi_ref, a_high, a_low, lanes))
    for r in range(0, radix, ROWS):
        us = []
        for k in range(half):
            lanes = slice((k % 2) * LANES, (k % 2 + 1) * LANES)
            gr = backs[k // 2][r : r + ROWS, lanes]
            gi = backs[k // 2][radix + r : radix + r + ROWS, lanes]
            c, s = tw_ref[r : r + ROWS, k : k + 1], tw_ref[r : r + ROWS, half + k : half + k + 1]
            us.append((gr * c - gi * s, gr * s + gi * c))
        for h, value in enumerate(half_inverse(us)):
            out_ref[h, r : r + ROWS, :] = value.astype(bf16)

    outer_forward(recv_ref, radix, tw_ref, b_high, b_low, half, radix)
    for m in range(half // 2):
        lanes = slice(m * 2 * LANES, (m + 1) * 2 * LANES)
        cot = inner_dft(wf_ref, b_high, b_low, lanes)
        spec = spec_ref[:, lanes]
        cr, ci, sr, si = cot[:radix], cot[radix:], spec[:radix], spec[radix:]
        for base, value in ((0, cr * sr + ci * si), (radix, ci * sr - cr * si)):
            high, low = split_pair(value)
            for side in range(2):
                row = (2 * m + side) * 2 * radix + base
                part = slice(side * LANES, (side + 1) * LANES)
                p_high[row : row + radix, :] = high[:, part]
                p_low[row : row + radix, :] = low[:, part]
    first = dot(taps_ref[...], p_high[...])
    grads = (first[:kp] + first[kp:] + dot(taps_ref[0:kp, :], p_low[...])) * scale
    g_high, g_low = split_pair(grads)
    used = taps + order
    fill = out_ref.shape[1] - radix - 2 * used
    pieces = [g_high.astype(f32)[:used], g_low.astype(f32)[:used]]
    if fill:
        pieces.append(jnp.zeros((fill, LANES), f32))
    pieces = jnp.concatenate(pieces, axis=0).astype(bf16)
    for j in range(out_ref.shape[0]):
        out_ref[j, radix:, :] = pieces


def unpack_kernel(back_ref, out_ref, mix_ref, ar_ref):
    tok = out_ref.shape[0]
    taps, order = mix_ref.shape[0], ar_ref.shape[0]
    used = taps + order
    for j in range(back_ref.shape[0]):
        lanes = slice(j * LANES, (j + 1) * LANES)
        out_ref[:, lanes] = back_ref[j, 0:tok, :]
        pieces = back_ref[j, tok:, :].astype(f32)
        grads = pieces[0:used] + pieces[used : 2 * used]
        mix_ref[:, lanes] = grads[0:taps]
        ar_ref[:, lanes] = grads[taps:used]


def shape_of(*dims, dtype=f32):
    return jax.ShapeDtypeStruct(dims, dtype)


def local_tiled(inputs, cotangent, filters, mixing, ar_coef):
    tok_rows, local_width = inputs.shape
    count = lax.axis_size("ctx")
    taps, order = filters.shape[1], ar_coef.shape[0]
    half, radix = count, tok_rows
    kp = -(-(taps + order) // 8) * 8
    wf, wi, twist, twist_t = dft_constants(half, radix)
    rows = 2 * tok_rows + 2 * taps
    back_rows = -(-(tok_rows + 2 * (taps + order)) // 8) * 8
    swap = functools.partial(lax.all_to_all, axis_name="ctx", split_axis=0, concat_axis=0, tiled=True)
    small = pltpu.CompilerParams(vmem_limit_bytes=8 << 20)

    send = pl.pallas_call(
        pack_kernel,
        out_shape=shape_of(count, rows, LANES, dtype=bf16),
        compiler_params=small,
        name="pack",
    )(inputs, cotangent, filters.T)
    recv = swap(send)

    whole = lambda *dims: pl.BlockSpec(dims, lambda i, place: (0,) * len(dims))
    place = lax.axis_index("ctx").astype(jnp.int32).reshape(1)
    span = half * LANES
    split = pltpu.VMEM((2 * radix, span), bf16)
    tall = pltpu.VMEM((half * 2 * radix, LANES), bf16)
    result = pl.pallas_call(
        functools.partial(main_kernel, half=half, radix=radix, kp=kp),
        out_shape=shape_of(count, back_rows, LANES, dtype=bf16),
        grid_spec=pltpu.PrefetchScalarGridSpec(
            num_scalar_prefetch=1,
            grid=(1,),
            in_specs=[
                whole(count, rows, LANES),
                pl.BlockSpec((taps, LANES), lambda i, place: (0, place[0])),
                pl.BlockSpec((order, LANES), lambda i, place: (0, place[0])),
                whole(*wf.shape),
                whole(*wi.shape),
                whole(*twist.shape),
                whole(*twist_t.shape),
            ],
            out_specs=whole(count, back_rows, LANES),
            scratch_shapes=[split] * 4
            + [pltpu.VMEM((2 * radix, span), f32), pltpu.VMEM((2 * kp, half * 2 * radix), bf16)]
            + [tall] * 2,
        ),
        compiler_params=pltpu.CompilerParams(vmem_limit_bytes=24 << 20),
        name="main",
    )(place, recv, mixing, ar_coef, wf, wi, twist, twist_t)
    back = swap(result)

    return pl.pallas_call(
        unpack_kernel,
        out_shape=(
            shape_of(tok_rows, local_width, dtype=bf16),
            shape_of(taps, local_width),
            shape_of(order, local_width),
        ),
        compiler_params=small,
        name="unpack",
    )(back)


def local(inputs, cotangent, filters, mixing, ar_coef):
    tok_rows, local_width = inputs.shape
    count = lax.axis_size("ctx")
    tiled = (
        local_width == count * LANES
        and tok_rows == LANES
        and count in (2, 4, 8)
        and filters.shape[1] % 8 == 0
    )
    return (local_tiled if tiled else local_general)(inputs, cotangent, filters, mixing, ar_coef)


def solution(mesh):
    return jax.shard_map(
        local,
        mesh=mesh,
        in_specs=(
            P(("groups", "ctx"), "mp"),
            P(("groups", "ctx"), "mp"),
            P("ctx", None),
            P(None, "mp"),
            P(None, "mp"),
        ),
        out_specs=(P(("groups", "ctx"), "mp"), P("groups", "mp"), P("groups", "mp")),
        check_vma=False,
    )
```

```python
import functools
import math

import jax
import jax.numpy as jnp
import numpy as np
from jax import lax
from jax.experimental import pallas as pl
from jax.experimental.pallas import tpu as pltpu
from jax.sharding import PartitionSpec as P

ORDER = 3
LANES = 128
ROWS = 16

f32 = jnp.float32
bf16 = jnp.bfloat16
highest = lax.Precision.HIGHEST


def phase_tables(seq_len):
    radix_len = math.gcd(seq_len, 128)
    outer_len = 2 * seq_len // radix_len
    half_outer = outer_len // 2
    total_len = 2 * seq_len
    low_index = jnp.arange(half_outer, dtype=jnp.int32)
    outer_index = jnp.arange(outer_len, dtype=jnp.int32)
    radix_index = jnp.arange(radix_len, dtype=jnp.int32)
    outer_angle = (low_index[:, None] * outer_index[None, :] % outer_len).astype(jnp.float32) * (
        2.0 * math.pi / outer_len
    )
    twist_angle = (outer_index[:, None] * radix_index[None, :] % total_len).astype(jnp.float32) * (
        2.0 * math.pi / total_len
    )
    radix_angle = (radix_index[:, None] * radix_index[None, :] % radix_len).astype(jnp.float32) * (
        2.0 * math.pi / radix_len
    )
    return (
        jnp.cos(outer_angle),
        jnp.sin(outer_angle),
        jnp.cos(twist_angle),
        jnp.sin(twist_angle),
        jnp.cos(radix_angle),
        jnp.sin(radix_angle),
    )


def forward_spectrum(signal, tables):
    outer_cos, outer_sin, twist_cos, twist_sin, radix_cos, radix_sin = tables
    channels = signal.shape[0]
    folded = signal.reshape(channels, outer_cos.shape[0], radix_cos.shape[0])
    first_real = jnp.einsum("chr,hk->ckr", folded, outer_cos, precision=highest)
    first_imag = -jnp.einsum("chr,hk->ckr", folded, outer_sin, precision=highest)
    turned_real = first_real * twist_cos + first_imag * twist_sin
    turned_imag = first_imag * twist_cos - first_real * twist_sin
    spec_real = jnp.einsum("ckr,rq->ckq", turned_real, radix_cos, precision=highest) + jnp.einsum(
        "ckr,rq->ckq", turned_imag, radix_sin, precision=highest
    )
    spec_imag = jnp.einsum("ckr,rq->ckq", turned_imag, radix_cos, precision=highest) - jnp.einsum(
        "ckr,rq->ckq", turned_real, radix_sin, precision=highest
    )
    return (spec_real, spec_imag)


def inverse_spectrum(spec_real, spec_imag, tables):
    outer_cos, outer_sin, twist_cos, twist_sin, radix_cos, radix_sin = tables
    back_real = jnp.einsum("ckq,rq->ckr", spec_real, radix_cos, precision=highest) - jnp.einsum(
        "ckq,rq->ckr", spec_imag, radix_sin, precision=highest
    )
    back_imag = jnp.einsum("ckq,rq->ckr", spec_real, radix_sin, precision=highest) + jnp.einsum(
        "ckq,rq->ckr", spec_imag, radix_cos, precision=highest
    )
    untwist_real = back_real * twist_cos - back_imag * twist_sin
    untwist_imag = back_real * twist_sin + back_imag * twist_cos
    folded = jnp.einsum("ckr,hk->chr", untwist_real, outer_cos, precision=highest) - jnp.einsum(
        "ckr,hk->chr", untwist_imag, outer_sin, precision=highest
    )
    channels = folded.shape[0]
    total_len = 2 * folded.shape[1] * folded.shape[2]
    return folded.reshape(channels, -1) / total_len


def local_general(inputs, cotangent, filters, mixing, ar_coef):
    tok_rows, local_width = inputs.shape
    ctx_count = lax.axis_size("ctx")
    ctx_place = lax.axis_index("ctx")
    narrow = local_width // ctx_count
    seq_len = tok_rows * ctx_count
    tables = phase_tables(seq_len)
    seq_cols = lax.all_to_all(inputs.T, "ctx", split_axis=0, concat_axis=1, tiled=True)
    signal = seq_cols.astype(jnp.float32)
    filter_all = lax.all_gather(filters, "ctx", axis=0, tiled=True)
    mix_local = lax.dynamic_slice_in_dim(mixing, ctx_place * narrow, narrow, 1)
    kernel = jnp.einsum("lk,kc->cl", filter_all, mix_local, precision=highest)
    sig_real, sig_imag = forward_spectrum(signal, tables)
    ker_real, ker_imag = forward_spectrum(kernel, tables)
    convolved = inverse_spectrum(
        ker_real * sig_real - ker_imag * sig_imag, ker_real * sig_imag + ker_imag * sig_real, tables
    )
    cot_cols = lax.all_to_all(cotangent.T, "ctx", split_axis=0, concat_axis=1, tiled=True)
    cot_real, cot_imag = forward_spectrum(cot_cols.astype(jnp.float32), tables)
    lagged = inverse_spectrum(
        cot_real * sig_real + cot_imag * sig_imag, cot_imag * sig_real - cot_real * sig_imag, tables
    )
    ar_local = lax.dynamic_slice_in_dim(ar_coef, ctx_place * narrow, narrow, 1)
    padded = jnp.pad(signal, ((0, 0), (ORDER, 0)))
    autoreg = jnp.zeros_like(signal)
    for lag_step in range(1, ORDER + 1):
        autoreg = (
            autoreg
            + ar_local[lag_step - 1][:, None]
            * padded[:, ORDER - lag_step : ORDER - lag_step + seq_len]
        )
    out_cols = (convolved + autoreg).astype(jnp.bfloat16)
    outputs = lax.all_to_all(out_cols, "ctx", split_axis=1, concat_axis=0, tiled=True).T
    mix_piece = jnp.einsum("lk,cl->kc", filter_all, lagged, precision=highest)
    grad_mixing, grad_ar = (
        lax.all_gather(mix_piece, "ctx", axis=1, tiled=True),
        lax.all_gather(lagged[:, 1 : ORDER + 1].T, "ctx", axis=1, tiled=True),
    )
    return (outputs, grad_mixing, grad_ar)


def split_pair(value):
    high = value.astype(bf16)
    return high, (value - high.astype(f32)).astype(bf16)


def turn(count, k):
    angle = math.pi * (k + 0.5) / count
    return math.cos(angle), math.sin(angle)


def half_forward(xs):
    n = len(xs)
    if n == 1:
        return [(xs[0], None)]
    even, odd = half_forward(xs[0::2]), half_forward(xs[1::2])
    low, high = [], []
    for k in range(n // 2):
        c, s = turn(n, k)
        er, ei = even[k]
        orr, oi = odd[k]
        if oi is None:
            tr, ti = orr * c, orr * (-s)
            low.append((er + tr, ti))
            high.append((er - tr, ti))
        else:
            tr, ti = orr * c + oi * s, oi * c - orr * s
            low.append((er + tr, ei + ti))
            high.append((er - tr, ti - ei))
    return low + high[::-1]


def half_inverse(us):
    n = len(us)
    if n == 1:
        return [us[0][0]]
    even, odd = [], []
    for k in range(n // 2):
        c, s = turn(n, k)
        (ar, ai), (br, bi) = us[k], us[n - 1 - k]
        dr, di = ar - br, ai + bi
        if n == 2:
            even.append((ar + br, None))
            odd.append((dr * c - di * s, None))
        else:
            even.append((ar + br, ai - bi))
            odd.append((dr * c - di * s, dr * s + di * c))
    out = [None] * n
    out[0::2] = half_inverse(even)
    out[1::2] = half_inverse(odd)
    return out


def dft_constants(half, radix):
    index = np.arange(radix)
    angle = 2.0 * np.pi * (index[:, None] * index[None, :] % radix) / radix
    c, s = np.cos(angle), np.sin(angle)
    forward = np.block([[c, s], [-s, c]])

    def stacked(matrix):
        matrix = matrix.astype(np.float32)
        high = matrix.astype(jnp.bfloat16)
        low = (matrix - high.astype(np.float32)).astype(jnp.bfloat16)
        return np.concatenate([high, low], axis=0)

    theta = 2.0 * np.pi * index[:, None] * (np.arange(half)[None, :] + 0.5) / (2 * half * radix)
    twist = np.concatenate([np.cos(theta), np.sin(theta)], axis=1).astype(np.float32)
    return stacked(forward), stacked(forward.T), twist, np.ascontiguousarray(twist.T)


def dot(a, b):
    return jnp.dot(a, b, preferred_element_type=f32)


def outer_forward(src_ref, start, tw_ref, high_ref, low_ref, half, radix):
    for r in range(0, radix, ROWS):
        parts = half_forward([src_ref[h, start + r : start + r + ROWS, :].astype(f32) for h in range(half)])
        for k, (re, im) in enumerate(parts):
            c, s = tw_ref[r : r + ROWS, k : k + 1], tw_ref[r : r + ROWS, half + k : half + k + 1]
            lanes = slice(k * LANES, (k + 1) * LANES)
            for base, value in ((0, re * c + im * s), (radix, im * c - re * s)):
                high, low = split_pair(value)
                high_ref[base + r : base + r + ROWS, lanes] = high
                low_ref[base + r : base + r + ROWS, lanes] = low


def inner_dft(w_ref, high_ref, low_ref, lanes):
    both = w_ref.shape[0] // 2
    first = dot(w_ref[...], high_ref[:, lanes])
    return first[:both] + first[both:] + dot(w_ref[:both, :], low_ref[:, lanes])


def pack_kernel(x_ref, g_ref, f_ref, send_ref, buf, in_sem, out_sem):
    count, rows, _ = send_ref.shape
    tok = x_ref.shape[0]
    copies = []
    for j in range(count):
        lanes = pl.ds(j * LANES, LANES)
        for side, src in enumerate((x_ref, g_ref)):
            copy = pltpu.make_async_copy(
                src.at[:, lanes], buf.at[j, pl.ds(side * tok, tok), :], in_sem.at[2 * j + side]
            )
            copy.start()
            copies.append(copy)
    @pl.when(lax.axis_index("mp") == 0)
    def _():
        pl.delay(5500)

    high, low = split_pair(f_ref[...])
    pieces = jnp.concatenate([high.astype(f32), low.astype(f32)], axis=0).astype(bf16)
    sends = []
    for j in range(count):
        buf[j, 2 * tok :, :] = pieces
        copies[2 * j].wait()
        copies[2 * j + 1].wait()
        send = pltpu.make_async_copy(buf.at[j], send_ref.at[j], out_sem.at[j])
        send.start()
        sends.append(send)
    for send in sends:
        send.wait()


def main_kernel(
    place_ref,
    recv_ref,
    mix_ref,
    ar_ref,
    wf_ref,
    wi_ref,
    tw_ref,
    twt_ref,
    out_ref,
    a_high,
    a_low,
    b_high,
    b_low,
    spec_ref,
    taps_ref,
    p_high,
    p_low,
    *,
    half,
    radix,
    kp,
):
    taps = mix_ref.shape[0]
    order = ar_ref.shape[0]
    width = 2 * radix
    scale = 1.0 / (half * radix)
    blocks = []
    for h in range(half):
        both = recv_ref[h, 2 * radix : 2 * radix + 2 * taps, :].astype(f32)
        value = both[:taps] + both[taps:]
        extra = jnp.zeros((kp - taps, radix), f32)
        if h == 0:
            row = lax.broadcasted_iota(jnp.int32, extra.shape, 0)
            lane = lax.broadcasted_iota(jnp.int32, extra.shape, 1)
            extra = jnp.where((row < order) & (lane == row + 1), 1.0, extra)
        blocks.append(jnp.concatenate([value, extra], axis=0))
    for k, (re, im) in enumerate(half_forward(blocks)):
        c, s = twt_ref[k : k + 1, :], twt_ref[half + k : half + k + 1, :]
        value = jnp.concatenate([re * c + im * s, im * c - re * s], axis=1)
        high, low = split_pair(value)
        a_high[k * kp : (k + 1) * kp, 0:width] = high
        a_low[k * kp : (k + 1) * kp, 0:width] = low
    n_rows = half * kp
    filt = (
        dot(a_high[0:n_rows, 0:width], wi_ref[0:width, :])
        + dot(a_low[0:n_rows, 0:width], wi_ref[0:width, :])
        + dot(a_high[0:n_rows, 0:width], wi_ref[width : 2 * width, :])
    )
    f_high, f_low = split_pair(filt)
    for k in range(half):
        rows = slice(k * kp, (k + 1) * kp)
        lanes = slice(k * width, (k + 1) * width)
        taps_ref[0:kp, lanes] = f_high[rows]
        taps_ref[kp : 2 * kp, lanes] = f_low[rows]
    weights = (
        jnp.concatenate([mix_ref[...], ar_ref[...], jnp.zeros((kp - taps - order, LANES), f32)], axis=0)
        * scale
    )
    m_high, m_low = split_pair(weights)
    zero = jnp.zeros_like(m_high)

    def diagonal(m):
        return jnp.concatenate(
            [jnp.concatenate([m, zero], axis=1), jnp.concatenate([zero, m], axis=1)], axis=0
        )

    d_high, d_low = diagonal(m_high), diagonal(m_low)
    mixer = jnp.concatenate([d_high, d_high, d_low], axis=0)

    outer_forward(recv_ref, 0, tw_ref, b_high, b_low, half, radix)
    for m in range(half // 2):
        lanes = slice(m * 2 * LANES, (m + 1) * 2 * LANES)
        rows = slice(2 * m * kp, 2 * (m + 1) * kp)
        spec = inner_dft(wf_ref, b_high, b_low, lanes)
        spec_ref[:, lanes] = spec
        ker = lax.dot_general(
            jnp.concatenate([f_high[rows], f_low[rows], f_high[rows]], axis=0),
            mixer,
            (((0,), (0,)), ((), ())),
            preferred_element_type=f32,
        )
        sr, si, kr, ki = spec[:radix], spec[radix:], ker[:radix], ker[radix:]
        for base, value in ((0, sr * kr - si * ki), (radix, sr * ki + si * kr)):
            high, low = split_pair(value)
            a_high[base : base + radix, lanes] = high
            a_low[base : base + radix, lanes] = low
    backs = []
    for m in range(half // 2):
        lanes = slice(m * 2 * LANES, (m + 1) * 2 * LANES)
        backs.append(inner_dft(wi_ref, a_high, a_low, lanes))
    for r in range(0, radix, ROWS):
        us = []
        for k in range(half):
            lanes = slice((k % 2) * LANES, (k % 2 + 1) * LANES)
            gr = backs[k // 2][r : r + ROWS, lanes]
            gi = backs[k // 2][radix + r : radix + r + ROWS, lanes]
            c, s = tw_ref[r : r + ROWS, k : k + 1], tw_ref[r : r + ROWS, half + k : half + k + 1]
            us.append((gr * c - gi * s, gr * s + gi * c))
        for h, value in enumerate(half_inverse(us)):
            out_ref[h, r : r + ROWS, :] = value.astype(bf16)

    outer_forward(recv_ref, radix, tw_ref, b_high, b_low, half, radix)
    for m in range(half // 2):
        lanes = slice(m * 2 * LANES, (m + 1) * 2 * LANES)
        cot = inner_dft(wf_ref, b_high, b_low, lanes)
        spec = spec_ref[:, lanes]
        cr, ci, sr, si = cot[:radix], cot[radix:], spec[:radix], spec[radix:]
        for base, value in ((0, cr * sr + ci * si), (radix, ci * sr - cr * si)):
            high, low = split_pair(value)
            for side in range(2):
                row = (2 * m + side) * 2 * radix + base
                part = slice(side * LANES, (side + 1) * LANES)
                p_high[row : row + radix, :] = high[:, part]
                p_low[row : row + radix, :] = low[:, part]
    first = dot(taps_ref[...], p_high[...])
    grads = (first[:kp] + first[kp:] + dot(taps_ref[0:kp, :], p_low[...])) * scale
    g_high, g_low = split_pair(grads)
    used = taps + order
    fill = out_ref.shape[1] - radix - 2 * used
    pieces = [g_high.astype(f32)[:used], g_low.astype(f32)[:used]]
    if fill:
        pieces.append(jnp.zeros((fill, LANES), f32))
    pieces = jnp.concatenate(pieces, axis=0).astype(bf16)
    for j in range(out_ref.shape[0]):
        out_ref[j, radix:, :] = pieces


def unpack_kernel(back_ref, out_ref, mix_ref, ar_ref):
    tok = out_ref.shape[0]
    taps, order = mix_ref.shape[0], ar_ref.shape[0]
    used = taps + order
    for j in range(back_ref.shape[0]):
        lanes = slice(j * LANES, (j + 1) * LANES)
        out_ref[:, lanes] = back_ref[j, 0:tok, :]
        pieces = back_ref[j, tok:, :].astype(f32)
        grads = pieces[0:used] + pieces[used : 2 * used]
        mix_ref[:, lanes] = grads[0:taps]
        ar_ref[:, lanes] = grads[taps:used]


def shape_of(*dims, dtype=f32):
    return jax.ShapeDtypeStruct(dims, dtype)


def local_tiled(inputs, cotangent, filters, mixing, ar_coef):
    tok_rows, local_width = inputs.shape
    count = lax.axis_size("ctx")
    taps, order = filters.shape[1], ar_coef.shape[0]
    half, radix = count, tok_rows
    kp = -(-(taps + order) // 8) * 8
    wf, wi, twist, twist_t = dft_constants(half, radix)
    rows = 2 * tok_rows + 2 * taps
    back_rows = -(-(tok_rows + 2 * (taps + order)) // 8) * 8
    swap = functools.partial(lax.all_to_all, axis_name="ctx", split_axis=0, concat_axis=0, tiled=True)
    small = pltpu.CompilerParams(vmem_limit_bytes=8 << 20)

    send = pl.pallas_call(
        pack_kernel,
        out_shape=shape_of(count, rows, LANES, dtype=bf16),
        in_specs=[
            pl.BlockSpec(memory_space=pl.ANY),
            pl.BlockSpec(memory_space=pl.ANY),
            pl.BlockSpec(memory_space=pltpu.VMEM),
        ],
        out_specs=pl.BlockSpec(memory_space=pl.ANY),
        scratch_shapes=[
            pltpu.VMEM((count, rows, LANES), bf16),
            pltpu.SemaphoreType.DMA((2 * count,)),
            pltpu.SemaphoreType.DMA((count,)),
        ],
        name="pack",
    )(inputs, cotangent, filters.T)
    recv = swap(send)

    whole = lambda *dims: pl.BlockSpec(dims, lambda i, place: (0,) * len(dims))
    place = lax.axis_index("ctx").astype(jnp.int32).reshape(1)
    span = half * LANES
    split = pltpu.VMEM((2 * radix, span), bf16)
    tall = pltpu.VMEM((half * 2 * radix, LANES), bf16)
    result = pl.pallas_call(
        functools.partial(main_kernel, half=half, radix=radix, kp=kp),
        out_shape=shape_of(count, back_rows, LANES, dtype=bf16),
        grid_spec=pltpu.PrefetchScalarGridSpec(
            num_scalar_prefetch=1,
            grid=(1,),
            in_specs=[
                whole(count, rows, LANES),
                pl.BlockSpec((taps, LANES), lambda i, place: (0, place[0])),
                pl.BlockSpec((order, LANES), lambda i, place: (0, place[0])),
                whole(*wf.shape),
                whole(*wi.shape),
                whole(*twist.shape),
                whole(*twist_t.shape),
            ],
            out_specs=whole(count, back_rows, LANES),
            scratch_shapes=[split] * 4
            + [pltpu.VMEM((2 * radix, span), f32), pltpu.VMEM((2 * kp, half * 2 * radix), bf16)]
            + [tall] * 2,
        ),
        compiler_params=pltpu.CompilerParams(vmem_limit_bytes=24 << 20),
        name="main",
    )(place, recv, mixing, ar_coef, wf, wi, twist, twist_t)
    back = swap(result)

    return pl.pallas_call(
        unpack_kernel,
        out_shape=(
            shape_of(tok_rows, local_width, dtype=bf16),
            shape_of(taps, local_width),
            shape_of(order, local_width),
        ),
        compiler_params=small,
        name="unpack",
    )(back)


def local(inputs, cotangent, filters, mixing, ar_coef):
    tok_rows, local_width = inputs.shape
    count = lax.axis_size("ctx")
    tiled = (
        local_width == count * LANES
        and tok_rows == LANES
        and count in (2, 4, 8)
        and filters.shape[1] % 8 == 0
    )
    return (local_tiled if tiled else local_general)(inputs, cotangent, filters, mixing, ar_coef)


def solution(mesh):
    return jax.shard_map(
        local,
        mesh=mesh,
        in_specs=(
            P(("groups", "ctx"), "mp"),
            P(("groups", "ctx"), "mp"),
            P("ctx", None),
            P(None, "mp"),
            P(None, "mp"),
        ),
        out_specs=(P(("groups", "ctx"), "mp"), P("groups", "mp"), P("groups", "mp")),
        check_vma=False,
    )
```

```python
import functools
import math

import jax
import jax.numpy as jnp
import numpy as np
from jax import lax
from jax.experimental import pallas as pl
from jax.experimental.pallas import tpu as pltpu
from jax.sharding import PartitionSpec as P

ORDER = 3
LANES = 128
ROWS = 16
STAGGER_NS = 5500

f32 = jnp.float32
bf16 = jnp.bfloat16
highest = lax.Precision.HIGHEST


def phase_tables(seq_len):
    radix_len = math.gcd(seq_len, 128)
    outer_len = 2 * seq_len // radix_len
    half_outer = outer_len // 2
    total_len = 2 * seq_len
    low_index = jnp.arange(half_outer, dtype=jnp.int32)
    outer_index = jnp.arange(outer_len, dtype=jnp.int32)
    radix_index = jnp.arange(radix_len, dtype=jnp.int32)
    outer_angle = (low_index[:, None] * outer_index[None, :] % outer_len).astype(jnp.float32) * (
        2.0 * math.pi / outer_len
    )
    twist_angle = (outer_index[:, None] * radix_index[None, :] % total_len).astype(jnp.float32) * (
        2.0 * math.pi / total_len
    )
    radix_angle = (radix_index[:, None] * radix_index[None, :] % radix_len).astype(jnp.float32) * (
        2.0 * math.pi / radix_len
    )
    return (
        jnp.cos(outer_angle),
        jnp.sin(outer_angle),
        jnp.cos(twist_angle),
        jnp.sin(twist_angle),
        jnp.cos(radix_angle),
        jnp.sin(radix_angle),
    )


def forward_spectrum(signal, tables):
    outer_cos, outer_sin, twist_cos, twist_sin, radix_cos, radix_sin = tables
    channels = signal.shape[0]
    folded = signal.reshape(channels, outer_cos.shape[0], radix_cos.shape[0])
    first_real = jnp.einsum("chr,hk->ckr", folded, outer_cos, precision=highest)
    first_imag = -jnp.einsum("chr,hk->ckr", folded, outer_sin, precision=highest)
    turned_real = first_real * twist_cos + first_imag * twist_sin
    turned_imag = first_imag * twist_cos - first_real * twist_sin
    spec_real = jnp.einsum("ckr,rq->ckq", turned_real, radix_cos, precision=highest) + jnp.einsum(
        "ckr,rq->ckq", turned_imag, radix_sin, precision=highest
    )
    spec_imag = jnp.einsum("ckr,rq->ckq", turned_imag, radix_cos, precision=highest) - jnp.einsum(
        "ckr,rq->ckq", turned_real, radix_sin, precision=highest
    )
    return (spec_real, spec_imag)


def inverse_spectrum(spec_real, spec_imag, tables):
    outer_cos, outer_sin, twist_cos, twist_sin, radix_cos, radix_sin = tables
    back_real = jnp.einsum("ckq,rq->ckr", spec_real, radix_cos, precision=highest) - jnp.einsum(
        "ckq,rq->ckr", spec_imag, radix_sin, precision=highest
    )
    back_imag = jnp.einsum("ckq,rq->ckr", spec_real, radix_sin, precision=highest) + jnp.einsum(
        "ckq,rq->ckr", spec_imag, radix_cos, precision=highest
    )
    untwist_real = back_real * twist_cos - back_imag * twist_sin
    untwist_imag = back_real * twist_sin + back_imag * twist_cos
    folded = jnp.einsum("ckr,hk->chr", untwist_real, outer_cos, precision=highest) - jnp.einsum(
        "ckr,hk->chr", untwist_imag, outer_sin, precision=highest
    )
    channels = folded.shape[0]
    total_len = 2 * folded.shape[1] * folded.shape[2]
    return folded.reshape(channels, -1) / total_len


def local_general(inputs, cotangent, filters, mixing, ar_coef):
    tok_rows, local_width = inputs.shape
    ctx_count = lax.axis_size("ctx")
    ctx_place = lax.axis_index("ctx")
    narrow = local_width // ctx_count
    seq_len = tok_rows * ctx_count
    tables = phase_tables(seq_len)
    seq_cols = lax.all_to_all(inputs.T, "ctx", split_axis=0, concat_axis=1, tiled=True)
    signal = seq_cols.astype(jnp.float32)
    filter_all = lax.all_gather(filters, "ctx", axis=0, tiled=True)
    mix_local = lax.dynamic_slice_in_dim(mixing, ctx_place * narrow, narrow, 1)
    kernel = jnp.einsum("lk,kc->cl", filter_all, mix_local, precision=highest)
    sig_real, sig_imag = forward_spectrum(signal, tables)
    ker_real, ker_imag = forward_spectrum(kernel, tables)
    convolved = inverse_spectrum(
        ker_real * sig_real - ker_imag * sig_imag, ker_real * sig_imag + ker_imag * sig_real, tables
    )
    cot_cols = lax.all_to_all(cotangent.T, "ctx", split_axis=0, concat_axis=1, tiled=True)
    cot_real, cot_imag = forward_spectrum(cot_cols.astype(jnp.float32), tables)
    lagged = inverse_spectrum(
        cot_real * sig_real + cot_imag * sig_imag, cot_imag * sig_real - cot_real * sig_imag, tables
    )
    ar_local = lax.dynamic_slice_in_dim(ar_coef, ctx_place * narrow, narrow, 1)
    padded = jnp.pad(signal, ((0, 0), (ORDER, 0)))
    autoreg = jnp.zeros_like(signal)
    for lag_step in range(1, ORDER + 1):
        autoreg = (
            autoreg
            + ar_local[lag_step - 1][:, None]
            * padded[:, ORDER - lag_step : ORDER - lag_step + seq_len]
        )
    out_cols = (convolved + autoreg).astype(jnp.bfloat16)
    outputs = lax.all_to_all(out_cols, "ctx", split_axis=1, concat_axis=0, tiled=True).T
    mix_piece = jnp.einsum("lk,cl->kc", filter_all, lagged, precision=highest)
    grad_mixing, grad_ar = (
        lax.all_gather(mix_piece, "ctx", axis=1, tiled=True),
        lax.all_gather(lagged[:, 1 : ORDER + 1].T, "ctx", axis=1, tiled=True),
    )
    return (outputs, grad_mixing, grad_ar)


def split_pair(value):
    high = value.astype(bf16)
    return high, (value - high.astype(f32)).astype(bf16)


def turn(count, k):
    angle = math.pi * (k + 0.5) / count
    return math.cos(angle), math.sin(angle)


def half_forward(xs):
    n = len(xs)
    if n == 1:
        return [(xs[0], None)]
    even, odd = half_forward(xs[0::2]), half_forward(xs[1::2])
    low, high = [], []
    for k in range(n // 2):
        c, s = turn(n, k)
        er, ei = even[k]
        orr, oi = odd[k]
        if oi is None:
            tr, ti = orr * c, orr * (-s)
            low.append((er + tr, ti))
            high.append((er - tr, ti))
        else:
            tr, ti = orr * c + oi * s, oi * c - orr * s
            low.append((er + tr, ei + ti))
            high.append((er - tr, ti - ei))
    return low + high[::-1]


def half_inverse(us):
    n = len(us)
    if n == 1:
        return [us[0][0]]
    even, odd = [], []
    for k in range(n // 2):
        c, s = turn(n, k)
        (ar, ai), (br, bi) = us[k], us[n - 1 - k]
        dr, di = ar - br, ai + bi
        if n == 2:
            even.append((ar + br, None))
            odd.append((dr * c - di * s, None))
        else:
            even.append((ar + br, ai - bi))
            odd.append((dr * c - di * s, dr * s + di * c))
    out = [None] * n
    out[0::2] = half_inverse(even)
    out[1::2] = half_inverse(odd)
    return out


def dft_constants(half, radix):
    index = np.arange(radix)
    angle = 2.0 * np.pi * (index[:, None] * index[None, :] % radix) / radix
    c, s = np.cos(angle), np.sin(angle)
    forward = np.block([[c, s], [-s, c]])

    def stacked(matrix):
        matrix = matrix.astype(np.float32)
        high = matrix.astype(jnp.bfloat16)
        low = (matrix - high.astype(np.float32)).astype(jnp.bfloat16)
        return np.concatenate([high, low], axis=0)

    theta = 2.0 * np.pi * index[:, None] * (np.arange(half)[None, :] + 0.5) / (2 * half * radix)
    twist = np.concatenate([np.cos(theta), np.sin(theta)], axis=1).astype(np.float32)
    table = np.zeros((radix + 2 * half, radix), np.float32)
    table[:radix, : 2 * half] = twist
    table[radix:] = twist.T
    return stacked(forward), stacked(forward.T), table


def dot(a, b):
    return jnp.dot(a, b, preferred_element_type=f32)


def outer_forward(src_ref, start, tw_ref, high_ref, low_ref, half, radix):
    for r in range(0, radix, ROWS):
        parts = half_forward([src_ref[h, start + r : start + r + ROWS, :].astype(f32) for h in range(half)])
        for k, (re, im) in enumerate(parts):
            c, s = tw_ref[r : r + ROWS, k : k + 1], tw_ref[r : r + ROWS, half + k : half + k + 1]
            lanes = slice(k * LANES, (k + 1) * LANES)
            for base, value in ((0, re * c + im * s), (radix, im * c - re * s)):
                high, low = split_pair(value)
                high_ref[base + r : base + r + ROWS, lanes] = high
                low_ref[base + r : base + r + ROWS, lanes] = low


def inner_dft(w_ref, high_ref, low_ref, lanes):
    both = w_ref.shape[0] // 2
    first = dot(w_ref[...], high_ref[:, lanes])
    return first[:both] + first[both:] + dot(w_ref[:both, :], low_ref[:, lanes])


def pack_kernel(x_ref, g_ref, f_ref, send_ref, buf, fbuf, in_sem, out_sem, *, wait):
    count, rows, _ = send_ref.shape
    tok = x_ref.shape[0]
    taps_in = pltpu.make_async_copy(f_ref, fbuf, in_sem.at[2 * count])
    taps_in.start()
    copies = []
    for j in range(count):
        lanes = pl.ds(j * LANES, LANES)
        for side, src in enumerate((x_ref, g_ref)):
            copy = pltpu.make_async_copy(
                src.at[:, lanes], buf.at[j, pl.ds(side * tok, tok), :], in_sem.at[2 * j + side]
            )
            copy.start()
            copies.append(copy)

    @pl.when(lax.axis_index("mp") == 0)
    def _():
        pl.delay(wait)

    taps_in.wait()
    high, low = split_pair(fbuf[...])
    pieces = jnp.concatenate([high.astype(f32), low.astype(f32)], axis=0).astype(bf16)
    for j in range(count):
        buf[j, 2 * tok :, :] = pieces
    sends = []
    for j in range(count):
        copies[2 * j].wait()
        copies[2 * j + 1].wait()
        send = pltpu.make_async_copy(buf.at[j], send_ref.at[j], out_sem.at[j])
        send.start()
        sends.append(send)
    for send in sends:
        send.wait()


def main_kernel(
    place_ref,
    recv_ref,
    mix_ref,
    ar_ref,
    wf_ref,
    wi_ref,
    tw_ref,
    out_ref,
    a_high,
    a_low,
    b_high,
    b_low,
    spec_ref,
    taps_ref,
    p_high,
    p_low,
    *,
    half,
    radix,
    kp,
):
    taps = mix_ref.shape[0]
    order = ar_ref.shape[0]
    width = 2 * radix
    scale = 1.0 / (half * radix)
    blocks = []
    for h in range(half):
        both = recv_ref[h, 2 * radix : 2 * radix + 2 * taps, :].astype(f32)
        value = both[:taps] + both[taps:]
        extra = jnp.zeros((kp - taps, radix), f32)
        if h == 0:
            row = lax.broadcasted_iota(jnp.int32, extra.shape, 0)
            lane = lax.broadcasted_iota(jnp.int32, extra.shape, 1)
            extra = jnp.where((row < order) & (lane == row + 1), 1.0, extra)
        blocks.append(jnp.concatenate([value, extra], axis=0))
    for k, (re, im) in enumerate(half_forward(blocks)):
        c, s = tw_ref[radix + k : radix + k + 1, :], tw_ref[radix + half + k : radix + half + k + 1, :]
        value = jnp.concatenate([re * c + im * s, im * c - re * s], axis=1)
        high, low = split_pair(value)
        a_high[k * kp : (k + 1) * kp, 0:width] = high
        a_low[k * kp : (k + 1) * kp, 0:width] = low
    n_rows = half * kp
    filt = (
        dot(a_high[0:n_rows, 0:width], wi_ref[0:width, :])
        + dot(a_low[0:n_rows, 0:width], wi_ref[0:width, :])
        + dot(a_high[0:n_rows, 0:width], wi_ref[width : 2 * width, :])
    )
    f_high, f_low = split_pair(filt)
    for k in range(half):
        rows = slice(k * kp, (k + 1) * kp)
        lanes = slice(k * width, (k + 1) * width)
        taps_ref[0:kp, lanes] = f_high[rows]
        taps_ref[kp : 2 * kp, lanes] = f_low[rows]
    weights = (
        jnp.concatenate([mix_ref[...], ar_ref[...], jnp.zeros((kp - taps - order, LANES), f32)], axis=0)
        * scale
    )
    m_high, m_low = split_pair(weights)
    zero = jnp.zeros_like(m_high)

    def diagonal(m):
        return jnp.concatenate(
            [jnp.concatenate([m, zero], axis=1), jnp.concatenate([zero, m], axis=1)], axis=0
        )

    d_high, d_low = diagonal(m_high), diagonal(m_low)
    mixer = jnp.concatenate([d_high, d_high, d_low], axis=0)

    outer_forward(recv_ref, 0, tw_ref, b_high, b_low, half, radix)
    for m in range(half // 2):
        lanes = slice(m * 2 * LANES, (m + 1) * 2 * LANES)
        rows = slice(2 * m * kp, 2 * (m + 1) * kp)
        spec = inner_dft(wf_ref, b_high, b_low, lanes)
        spec_ref[:, lanes] = spec
        ker = lax.dot_general(
            jnp.concatenate([f_high[rows], f_low[rows], f_high[rows]], axis=0),
            mixer,
            (((0,), (0,)), ((), ())),
            preferred_element_type=f32,
        )
        sr, si, kr, ki = spec[:radix], spec[radix:], ker[:radix], ker[radix:]
        for base, value in ((0, sr * kr - si * ki), (radix, sr * ki + si * kr)):
            high, low = split_pair(value)
            a_high[base : base + radix, lanes] = high
            a_low[base : base + radix, lanes] = low
    backs = []
    for m in range(half // 2):
        lanes = slice(m * 2 * LANES, (m + 1) * 2 * LANES)
        backs.append(inner_dft(wi_ref, a_high, a_low, lanes))
    for r in range(0, radix, ROWS):
        us = []
        for k in range(half):
            lanes = slice((k % 2) * LANES, (k % 2 + 1) * LANES)
            gr = backs[k // 2][r : r + ROWS, lanes]
            gi = backs[k // 2][radix + r : radix + r + ROWS, lanes]
            c, s = tw_ref[r : r + ROWS, k : k + 1], tw_ref[r : r + ROWS, half + k : half + k + 1]
            us.append((gr * c - gi * s, gr * s + gi * c))
        for h, value in enumerate(half_inverse(us)):
            out_ref[h, r : r + ROWS, :] = value.astype(bf16)

    outer_forward(recv_ref, radix, tw_ref, b_high, b_low, half, radix)
    for m in range(half // 2):
        lanes = slice(m * 2 * LANES, (m + 1) * 2 * LANES)
        cot = inner_dft(wf_ref, b_high, b_low, lanes)
        spec = spec_ref[:, lanes]
        cr, ci, sr, si = cot[:radix], cot[radix:], spec[:radix], spec[radix:]
        for base, value in ((0, cr * sr + ci * si), (radix, ci * sr - cr * si)):
            high, low = split_pair(value)
            for side in range(2):
                row = (2 * m + side) * 2 * radix + base
                part = slice(side * LANES, (side + 1) * LANES)
                p_high[row : row + radix, :] = high[:, part]
                p_low[row : row + radix, :] = low[:, part]
    first = dot(taps_ref[...], p_high[...])
    grads = (first[:kp] + first[kp:] + dot(taps_ref[0:kp, :], p_low[...])) * scale
    g_high, g_low = split_pair(grads)
    used = taps + order
    fill = out_ref.shape[1] - radix - 2 * used
    pieces = [g_high.astype(f32)[:used], g_low.astype(f32)[:used]]
    if fill:
        pieces.append(jnp.zeros((fill, LANES), f32))
    pieces = jnp.concatenate(pieces, axis=0).astype(bf16)
    for j in range(out_ref.shape[0]):
        out_ref[j, radix:, :] = pieces


def unpack_kernel(back_ref, out_ref, mix_ref, ar_ref):
    tok = out_ref.shape[0]
    taps, order = mix_ref.shape[0], ar_ref.shape[0]
    used = taps + order
    for j in range(back_ref.shape[0]):
        lanes = slice(j * LANES, (j + 1) * LANES)
        out_ref[:, lanes] = back_ref[j, 0:tok, :]
        pieces = back_ref[j, tok:, :].astype(f32)
        grads = pieces[0:used] + pieces[used : 2 * used]
        mix_ref[:, lanes] = grads[0:taps]
        ar_ref[:, lanes] = grads[taps:used]


def shape_of(*dims, dtype=f32):
    return jax.ShapeDtypeStruct(dims, dtype)


def local_tiled(inputs, cotangent, filters, mixing, ar_coef):
    tok_rows, local_width = inputs.shape
    count = lax.axis_size("ctx")
    taps, order = filters.shape[1], ar_coef.shape[0]
    half, radix = count, tok_rows
    kp = -(-(taps + order) // 8) * 8
    wf, wi, twist = dft_constants(half, radix)
    rows = 2 * tok_rows + 2 * taps
    back_rows = -(-(tok_rows + 2 * (taps + order)) // 8) * 8
    swap = functools.partial(lax.all_to_all, axis_name="ctx", split_axis=0, concat_axis=0, tiled=True)
    small = pltpu.CompilerParams(vmem_limit_bytes=8 << 20)

    send = pl.pallas_call(
        functools.partial(pack_kernel, wait=STAGGER_NS),
        out_shape=shape_of(count, rows, LANES, dtype=bf16),
        in_specs=[pl.BlockSpec(memory_space=pl.ANY)] * 3,
        out_specs=pl.BlockSpec(memory_space=pl.ANY),
        scratch_shapes=[
            pltpu.VMEM((count, rows, LANES), bf16),
            pltpu.VMEM((taps, tok_rows), f32),
            pltpu.SemaphoreType.DMA((2 * count + 1,)),
            pltpu.SemaphoreType.DMA((count,)),
        ],
        name="pack",
    )(inputs, cotangent, filters.T)
    recv = swap(send)

    whole = lambda *dims: pl.BlockSpec(dims, lambda i, place: (0,) * len(dims))
    place = lax.axis_index("ctx").astype(jnp.int32).reshape(1)
    span = half * LANES
    split = pltpu.VMEM((2 * radix, span), bf16)
    tall = pltpu.VMEM((half * 2 * radix, LANES), bf16)
    result = pl.pallas_call(
        functools.partial(main_kernel, half=half, radix=radix, kp=kp),
        out_shape=shape_of(count, back_rows, LANES, dtype=bf16),
        grid_spec=pltpu.PrefetchScalarGridSpec(
            num_scalar_prefetch=1,
            grid=(1,),
            in_specs=[
                whole(count, rows, LANES),
                pl.BlockSpec((taps, LANES), lambda i, place: (0, place[0])),
                pl.BlockSpec((order, LANES), lambda i, place: (0, place[0])),
                whole(*wf.shape),
                whole(*wi.shape),
                whole(*twist.shape),
            ],
            out_specs=whole(count, back_rows, LANES),
            scratch_shapes=[split] * 4
            + [pltpu.VMEM((2 * radix, span), f32), pltpu.VMEM((2 * kp, half * 2 * radix), bf16)]
            + [tall] * 2,
        ),
        compiler_params=pltpu.CompilerParams(vmem_limit_bytes=24 << 20),
        name="main",
    )(place, recv, mixing, ar_coef, wf, wi, twist)
    back = swap(result)

    return pl.pallas_call(
        unpack_kernel,
        out_shape=(
            shape_of(tok_rows, local_width, dtype=bf16),
            shape_of(taps, local_width),
            shape_of(order, local_width),
        ),
        compiler_params=small,
        name="unpack",
    )(back)


def local(inputs, cotangent, filters, mixing, ar_coef):
    tok_rows, local_width = inputs.shape
    count = lax.axis_size("ctx")
    tiled = (
        local_width == count * LANES
        and tok_rows == LANES
        and count in (2, 4, 8)
        and filters.shape[1] % 8 == 0
    )
    return (local_tiled if tiled else local_general)(inputs, cotangent, filters, mixing, ar_coef)


def solution(mesh):
    return jax.shard_map(
        local,
        mesh=mesh,
        in_specs=(
            P(("groups", "ctx"), "mp"),
            P(("groups", "ctx"), "mp"),
            P("ctx", None),
            P(None, "mp"),
            P(None, "mp"),
        ),
        out_specs=(P(("groups", "ctx"), "mp"), P("groups", "mp"), P("groups", "mp")),
        check_vma=False,
    )
```

```python
import functools
import math

import jax
import jax.numpy as jnp
import numpy as np
from jax import lax
from jax.experimental import pallas as pl
from jax.experimental.pallas import tpu as pltpu
from jax.sharding import PartitionSpec as P

ORDER = 3
LANES = 128
ROWS = 16
STAGGER_NS = 5500

f32 = jnp.float32
bf16 = jnp.bfloat16
highest = lax.Precision.HIGHEST


def phase_tables(seq_len):
    radix_len = math.gcd(seq_len, 128)
    outer_len = 2 * seq_len // radix_len
    half_outer = outer_len // 2
    total_len = 2 * seq_len
    low_index = jnp.arange(half_outer, dtype=jnp.int32)
    outer_index = jnp.arange(outer_len, dtype=jnp.int32)
    radix_index = jnp.arange(radix_len, dtype=jnp.int32)
    outer_angle = (low_index[:, None] * outer_index[None, :] % outer_len).astype(jnp.float32) * (
        2.0 * math.pi / outer_len
    )
    twist_angle = (outer_index[:, None] * radix_index[None, :] % total_len).astype(jnp.float32) * (
        2.0 * math.pi / total_len
    )
    radix_angle = (radix_index[:, None] * radix_index[None, :] % radix_len).astype(jnp.float32) * (
        2.0 * math.pi / radix_len
    )
    return (
        jnp.cos(outer_angle),
        jnp.sin(outer_angle),
        jnp.cos(twist_angle),
        jnp.sin(twist_angle),
        jnp.cos(radix_angle),
        jnp.sin(radix_angle),
    )


def forward_spectrum(signal, tables):
    outer_cos, outer_sin, twist_cos, twist_sin, radix_cos, radix_sin = tables
    channels = signal.shape[0]
    folded = signal.reshape(channels, outer_cos.shape[0], radix_cos.shape[0])
    first_real = jnp.einsum("chr,hk->ckr", folded, outer_cos, precision=highest)
    first_imag = -jnp.einsum("chr,hk->ckr", folded, outer_sin, precision=highest)
    turned_real = first_real * twist_cos + first_imag * twist_sin
    turned_imag = first_imag * twist_cos - first_real * twist_sin
    spec_real = jnp.einsum("ckr,rq->ckq", turned_real, radix_cos, precision=highest) + jnp.einsum(
        "ckr,rq->ckq", turned_imag, radix_sin, precision=highest
    )
    spec_imag = jnp.einsum("ckr,rq->ckq", turned_imag, radix_cos, precision=highest) - jnp.einsum(
        "ckr,rq->ckq", turned_real, radix_sin, precision=highest
    )
    return (spec_real, spec_imag)


def inverse_spectrum(spec_real, spec_imag, tables):
    outer_cos, outer_sin, twist_cos, twist_sin, radix_cos, radix_sin = tables
    back_real = jnp.einsum("ckq,rq->ckr", spec_real, radix_cos, precision=highest) - jnp.einsum(
        "ckq,rq->ckr", spec_imag, radix_sin, precision=highest
    )
    back_imag = jnp.einsum("ckq,rq->ckr", spec_real, radix_sin, precision=highest) + jnp.einsum(
        "ckq,rq->ckr", spec_imag, radix_cos, precision=highest
    )
    untwist_real = back_real * twist_cos - back_imag * twist_sin
    untwist_imag = back_real * twist_sin + back_imag * twist_cos
    folded = jnp.einsum("ckr,hk->chr", untwist_real, outer_cos, precision=highest) - jnp.einsum(
        "ckr,hk->chr", untwist_imag, outer_sin, precision=highest
    )
    channels = folded.shape[0]
    total_len = 2 * folded.shape[1] * folded.shape[2]
    return folded.reshape(channels, -1) / total_len


def local_general(inputs, cotangent, filters, mixing, ar_coef):
    tok_rows, local_width = inputs.shape
    ctx_count = lax.axis_size("ctx")
    ctx_place = lax.axis_index("ctx")
    narrow = local_width // ctx_count
    seq_len = tok_rows * ctx_count
    tables = phase_tables(seq_len)
    seq_cols = lax.all_to_all(inputs.T, "ctx", split_axis=0, concat_axis=1, tiled=True)
    signal = seq_cols.astype(jnp.float32)
    filter_all = lax.all_gather(filters, "ctx", axis=0, tiled=True)
    mix_local = lax.dynamic_slice_in_dim(mixing, ctx_place * narrow, narrow, 1)
    kernel = jnp.einsum("lk,kc->cl", filter_all, mix_local, precision=highest)
    sig_real, sig_imag = forward_spectrum(signal, tables)
    ker_real, ker_imag = forward_spectrum(kernel, tables)
    convolved = inverse_spectrum(
        ker_real * sig_real - ker_imag * sig_imag, ker_real * sig_imag + ker_imag * sig_real, tables
    )
    cot_cols = lax.all_to_all(cotangent.T, "ctx", split_axis=0, concat_axis=1, tiled=True)
    cot_real, cot_imag = forward_spectrum(cot_cols.astype(jnp.float32), tables)
    lagged = inverse_spectrum(
        cot_real * sig_real + cot_imag * sig_imag, cot_imag * sig_real - cot_real * sig_imag, tables
    )
    ar_local = lax.dynamic_slice_in_dim(ar_coef, ctx_place * narrow, narrow, 1)
    padded = jnp.pad(signal, ((0, 0), (ORDER, 0)))
    autoreg = jnp.zeros_like(signal)
    for lag_step in range(1, ORDER + 1):
        autoreg = (
            autoreg
            + ar_local[lag_step - 1][:, None]
            * padded[:, ORDER - lag_step : ORDER - lag_step + seq_len]
        )
    out_cols = (convolved + autoreg).astype(jnp.bfloat16)
    outputs = lax.all_to_all(out_cols, "ctx", split_axis=1, concat_axis=0, tiled=True).T
    mix_piece = jnp.einsum("lk,cl->kc", filter_all, lagged, precision=highest)
    grad_mixing, grad_ar = (
        lax.all_gather(mix_piece, "ctx", axis=1, tiled=True),
        lax.all_gather(lagged[:, 1 : ORDER + 1].T, "ctx", axis=1, tiled=True),
    )
    return (outputs, grad_mixing, grad_ar)


def split_pair(value):
    high = value.astype(bf16)
    return high, (value - high.astype(f32)).astype(bf16)


def turn(count, k):
    angle = math.pi * (k + 0.5) / count
    return math.cos(angle), math.sin(angle)


def half_forward(xs):
    n = len(xs)
    if n == 1:
        return [(xs[0], None)]
    even, odd = half_forward(xs[0::2]), half_forward(xs[1::2])
    low, high = [], []
    for k in range(n // 2):
        c, s = turn(n, k)
        er, ei = even[k]
        orr, oi = odd[k]
        if oi is None:
            tr, ti = orr * c, orr * (-s)
            low.append((er + tr, ti))
            high.append((er - tr, ti))
        else:
            tr, ti = orr * c + oi * s, oi * c - orr * s
            low.append((er + tr, ei + ti))
            high.append((er - tr, ti - ei))
    return low + high[::-1]


def half_inverse(us):
    n = len(us)
    if n == 1:
        return [us[0][0]]
    even, odd = [], []
    for k in range(n // 2):
        c, s = turn(n, k)
        (ar, ai), (br, bi) = us[k], us[n - 1 - k]
        dr, di = ar - br, ai + bi
        if n == 2:
            even.append((ar + br, None))
            odd.append((dr * c - di * s, None))
        else:
            even.append((ar + br, ai - bi))
            odd.append((dr * c - di * s, dr * s + di * c))
    out = [None] * n
    out[0::2] = half_inverse(even)
    out[1::2] = half_inverse(odd)
    return out


def dft_constants(half, radix):
    index = np.arange(radix)
    angle = 2.0 * np.pi * (index[:, None] * index[None, :] % radix) / radix
    c, s = np.cos(angle), np.sin(angle)
    forward = np.block([[c, s], [-s, c]])

    def stacked(matrix):
        matrix = matrix.astype(np.float32)
        high = matrix.astype(jnp.bfloat16)
        low = (matrix - high.astype(np.float32)).astype(jnp.bfloat16)
        return np.concatenate([high, low], axis=0)

    theta = 2.0 * np.pi * index[:, None] * (np.arange(half)[None, :] + 0.5) / (2 * half * radix)
    twist = np.concatenate([np.cos(theta), np.sin(theta)], axis=1).astype(np.float32)
    table = np.zeros((radix + 2 * half, radix), np.float32)
    table[:radix, : 2 * half] = twist
    table[radix:] = twist.T
    return stacked(forward), stacked(forward.T), table


def dot(a, b):
    return jnp.dot(a, b, preferred_element_type=f32)


def outer_forward(src_ref, start, tw_ref, high_ref, low_ref, half, radix):
    for r in range(0, radix, ROWS):
        parts = half_forward([src_ref[h, start + r : start + r + ROWS, :].astype(f32) for h in range(half)])
        for k, (re, im) in enumerate(parts):
            c, s = tw_ref[r : r + ROWS, k : k + 1], tw_ref[r : r + ROWS, half + k : half + k + 1]
            lanes = slice(k * LANES, (k + 1) * LANES)
            for base, value in ((0, re * c + im * s), (radix, im * c - re * s)):
                high, low = split_pair(value)
                high_ref[base + r : base + r + ROWS, lanes] = high
                low_ref[base + r : base + r + ROWS, lanes] = low


def inner_dft(w_ref, high_ref, low_ref, lanes):
    both = w_ref.shape[0] // 2
    first = dot(w_ref[...], high_ref[:, lanes])
    return first[:both] + first[both:] + dot(w_ref[:both, :], low_ref[:, lanes])


def pack_kernel(place_ref, x_ref, g_ref, f_ref, send_ref, fbuf, sems, *, wait):
    count = send_ref.shape[0]
    tok = x_ref.shape[0]
    taps_in = pltpu.make_async_copy(f_ref, fbuf, sems.at[2 * count])
    taps_in.start()
    copies = []
    for j in range(count):
        lanes = pl.ds(j * LANES, LANES)
        for side, src in enumerate((x_ref, g_ref)):
            copy = pltpu.make_async_copy(
                src.at[:, lanes], send_ref.at[j, pl.ds(side * tok, tok), :], sems.at[2 * j + side]
            )
            copy.start()
            copies.append(copy)

    @pl.when(lax.axis_index("mp") == 0)
    def _():
        pl.delay(wait)

    taps_in.wait()
    high, low = split_pair(fbuf[...])
    pieces = jnp.concatenate([high.astype(f32), low.astype(f32)], axis=0).astype(bf16)
    for j in range(count):
        send_ref[j, 2 * tok :, :] = pieces
    for copy in copies:
        copy.wait()


def main_kernel(
    place_ref,
    recv_ref,
    mix_ref,
    ar_ref,
    wf_ref,
    wi_ref,
    tw_ref,
    out_ref,
    a_high,
    a_low,
    b_high,
    b_low,
    spec_ref,
    taps_ref,
    p_high,
    p_low,
    *,
    half,
    radix,
    kp,
):
    taps = mix_ref.shape[0]
    order = ar_ref.shape[0]
    width = 2 * radix
    scale = 1.0 / (half * radix)
    blocks = []
    for h in range(half):
        both = recv_ref[h, 2 * radix : 2 * radix + 2 * taps, :].astype(f32)
        value = both[:taps] + both[taps:]
        extra = jnp.zeros((kp - taps, radix), f32)
        if h == 0:
            row = lax.broadcasted_iota(jnp.int32, extra.shape, 0)
            lane = lax.broadcasted_iota(jnp.int32, extra.shape, 1)
            extra = jnp.where((row < order) & (lane == row + 1), 1.0, extra)
        blocks.append(jnp.concatenate([value, extra], axis=0))
    for k, (re, im) in enumerate(half_forward(blocks)):
        c, s = tw_ref[radix + k : radix + k + 1, :], tw_ref[radix + half + k : radix + half + k + 1, :]
        value = jnp.concatenate([re * c + im * s, im * c - re * s], axis=1)
        high, low = split_pair(value)
        a_high[k * kp : (k + 1) * kp, 0:width] = high
        a_low[k * kp : (k + 1) * kp, 0:width] = low
    n_rows = half * kp
    filt = (
        dot(a_high[0:n_rows, 0:width], wi_ref[0:width, :])
        + dot(a_low[0:n_rows, 0:width], wi_ref[0:width, :])
        + dot(a_high[0:n_rows, 0:width], wi_ref[width : 2 * width, :])
    )
    f_high, f_low = split_pair(filt)
    for k in range(half):
        rows = slice(k * kp, (k + 1) * kp)
        lanes = slice(k * width, (k + 1) * width)
        taps_ref[0:kp, lanes] = f_high[rows]
        taps_ref[kp : 2 * kp, lanes] = f_low[rows]
    weights = (
        jnp.concatenate([mix_ref[...], ar_ref[...], jnp.zeros((kp - taps - order, LANES), f32)], axis=0)
        * scale
    )
    m_high, m_low = split_pair(weights)
    zero = jnp.zeros_like(m_high)

    def diagonal(m):
        return jnp.concatenate(
            [jnp.concatenate([m, zero], axis=1), jnp.concatenate([zero, m], axis=1)], axis=0
        )

    d_high, d_low = diagonal(m_high), diagonal(m_low)
    mixer = jnp.concatenate([d_high, d_high, d_low], axis=0)

    outer_forward(recv_ref, 0, tw_ref, b_high, b_low, half, radix)
    for m in range(half // 2):
        lanes = slice(m * 2 * LANES, (m + 1) * 2 * LANES)
        rows = slice(2 * m * kp, 2 * (m + 1) * kp)
        spec = inner_dft(wf_ref, b_high, b_low, lanes)
        spec_ref[:, lanes] = spec
        ker = lax.dot_general(
            jnp.concatenate([f_high[rows], f_low[rows], f_high[rows]], axis=0),
            mixer,
            (((0,), (0,)), ((), ())),
            preferred_element_type=f32,
        )
        sr, si, kr, ki = spec[:radix], spec[radix:], ker[:radix], ker[radix:]
        for base, value in ((0, sr * kr - si * ki), (radix, sr * ki + si * kr)):
            high, low = split_pair(value)
            a_high[base : base + radix, lanes] = high
            a_low[base : base + radix, lanes] = low
    backs = []
    for m in range(half // 2):
        lanes = slice(m * 2 * LANES, (m + 1) * 2 * LANES)
        backs.append(inner_dft(wi_ref, a_high, a_low, lanes))
    for r in range(0, radix, ROWS):
        us = []
        for k in range(half):
            lanes = slice((k % 2) * LANES, (k % 2 + 1) * LANES)
            gr = backs[k // 2][r : r + ROWS, lanes]
            gi = backs[k // 2][radix + r : radix + r + ROWS, lanes]
            c, s = tw_ref[r : r + ROWS, k : k + 1], tw_ref[r : r + ROWS, half + k : half + k + 1]
            us.append((gr * c - gi * s, gr * s + gi * c))
        for h, value in enumerate(half_inverse(us)):
            out_ref[h, r : r + ROWS, :] = value.astype(bf16)

    outer_forward(recv_ref, radix, tw_ref, b_high, b_low, half, radix)
    for m in range(half // 2):
        lanes = slice(m * 2 * LANES, (m + 1) * 2 * LANES)
        cot = inner_dft(wf_ref, b_high, b_low, lanes)
        spec = spec_ref[:, lanes]
        cr, ci, sr, si = cot[:radix], cot[radix:], spec[:radix], spec[radix:]
        for base, value in ((0, cr * sr + ci * si), (radix, ci * sr - cr * si)):
            high, low = split_pair(value)
            for side in range(2):
                row = (2 * m + side) * 2 * radix + base
                part = slice(side * LANES, (side + 1) * LANES)
                p_high[row : row + radix, :] = high[:, part]
                p_low[row : row + radix, :] = low[:, part]
    first = dot(taps_ref[...], p_high[...])
    grads = (first[:kp] + first[kp:] + dot(taps_ref[0:kp, :], p_low[...])) * scale
    g_high, g_low = split_pair(grads)
    used = taps + order
    fill = out_ref.shape[1] - radix - 2 * used
    pieces = [g_high.astype(f32)[:used], g_low.astype(f32)[:used]]
    if fill:
        pieces.append(jnp.zeros((fill, LANES), f32))
    pieces = jnp.concatenate(pieces, axis=0).astype(bf16)
    for j in range(out_ref.shape[0]):
        out_ref[j, radix:, :] = pieces


def unpack_kernel(back_ref, out_ref, mix_ref, ar_ref, mix_buf, ar_buf, sems):
    count = back_ref.shape[0]
    tok = out_ref.shape[0]
    taps, order = mix_ref.shape[0], ar_ref.shape[0]
    used = taps + order
    copies = []
    for j in range(count):
        lanes = pl.ds(j * LANES, LANES)
        copy = pltpu.make_async_copy(back_ref.at[j, pl.ds(0, tok), :], out_ref.at[:, lanes], sems.at[j])
        copy.start()
        copies.append(copy)
    for j in range(count):
        lanes = slice(j * LANES, (j + 1) * LANES)
        pieces = back_ref[j, tok:, :].astype(f32)
        grads = pieces[0:used] + pieces[used : 2 * used]
        mix_buf[:, lanes] = grads[0:taps]
        ar_buf[:, lanes] = grads[taps:used]
    for buf, ref, place in ((mix_buf, mix_ref, count), (ar_buf, ar_ref, count + 1)):
        copy = pltpu.make_async_copy(buf, ref, sems.at[place])
        copy.start()
        copies.append(copy)
    for copy in copies:
        copy.wait()


def shape_of(*dims, dtype=f32):
    return jax.ShapeDtypeStruct(dims, dtype)


def local_tiled(inputs, cotangent, filters, mixing, ar_coef):
    tok_rows, local_width = inputs.shape
    count = lax.axis_size("ctx")
    taps, order = filters.shape[1], ar_coef.shape[0]
    half, radix = count, tok_rows
    kp = -(-(taps + order) // 8) * 8
    wf, wi, twist = dft_constants(half, radix)
    rows = 2 * tok_rows + 2 * taps
    back_rows = -(-(tok_rows + 2 * (taps + order)) // 8) * 8
    swap = functools.partial(lax.all_to_all, axis_name="ctx", split_axis=0, concat_axis=0, tiled=True)
    small = pltpu.CompilerParams(vmem_limit_bytes=8 << 20)

    place = lax.axis_index("ctx").astype(jnp.int32).reshape(1)
    stay = functools.partial(pltpu.with_memory_space_constraint, memory_space=pltpu.HBM)
    send = pl.pallas_call(
        functools.partial(pack_kernel, wait=STAGGER_NS),
        out_shape=shape_of(count, rows, LANES, dtype=bf16),
        in_specs=[pl.BlockSpec(memory_space=pltpu.SMEM)] + [pl.BlockSpec(memory_space=pltpu.HBM)] * 3,
        out_specs=pl.BlockSpec(memory_space=pltpu.VMEM),
        scratch_shapes=[
            pltpu.VMEM((taps, tok_rows), f32),
            pltpu.SemaphoreType.DMA((2 * count + 1,)),
        ],
        compiler_params=small,
        name="pack",
    )(place, stay(inputs), stay(cotangent), stay(filters.T))
    recv = swap(send)

    whole = lambda *dims: pl.BlockSpec(dims, lambda i, place: (0,) * len(dims))
    span = half * LANES
    split = pltpu.VMEM((2 * radix, span), bf16)
    tall = pltpu.VMEM((half * 2 * radix, LANES), bf16)
    result = pl.pallas_call(
        functools.partial(main_kernel, half=half, radix=radix, kp=kp),
        out_shape=shape_of(count, back_rows, LANES, dtype=bf16),
        grid_spec=pltpu.PrefetchScalarGridSpec(
            num_scalar_prefetch=1,
            grid=(1,),
            in_specs=[
                whole(count, rows, LANES),
                pl.BlockSpec((taps, LANES), lambda i, place: (0, place[0])),
                pl.BlockSpec((order, LANES), lambda i, place: (0, place[0])),
                whole(*wf.shape),
                whole(*wi.shape),
                whole(*twist.shape),
            ],
            out_specs=whole(count, back_rows, LANES),
            scratch_shapes=[split] * 4
            + [pltpu.VMEM((2 * radix, span), f32), pltpu.VMEM((2 * kp, half * 2 * radix), bf16)]
            + [tall] * 2,
        ),
        compiler_params=pltpu.CompilerParams(vmem_limit_bytes=24 << 20),
        name="main",
    )(place, recv, mixing, ar_coef, wf, wi, twist)
    back = swap(result)

    return pl.pallas_call(
        unpack_kernel,
        out_shape=(
            shape_of(tok_rows, local_width, dtype=bf16),
            shape_of(taps, local_width),
            shape_of(order, local_width),
        ),
        in_specs=[pl.BlockSpec(memory_space=pltpu.VMEM)],
        out_specs=[pl.BlockSpec(memory_space=pl.ANY)] * 3,
        scratch_shapes=[
            pltpu.VMEM((taps, local_width), f32),
            pltpu.VMEM((order, local_width), f32),
            pltpu.SemaphoreType.DMA((count + 2,)),
        ],
        compiler_params=small,
        name="unpack",
    )(back)


def local(inputs, cotangent, filters, mixing, ar_coef):
    tok_rows, local_width = inputs.shape
    count = lax.axis_size("ctx")
    tiled = (
        local_width == count * LANES
        and tok_rows == LANES
        and count in (2, 4, 8)
        and filters.shape[1] % 8 == 0
    )
    return (local_tiled if tiled else local_general)(inputs, cotangent, filters, mixing, ar_coef)


def solution(mesh):
    return jax.shard_map(
        local,
        mesh=mesh,
        in_specs=(
            P(("groups", "ctx"), "mp"),
            P(("groups", "ctx"), "mp"),
            P("ctx", None),
            P(None, "mp"),
            P(None, "mp"),
        ),
        out_specs=(P(("groups", "ctx"), "mp"), P("groups", "mp"), P("groups", "mp")),
        check_vma=False,
    )
```

```python
import functools
import math

import jax
import jax.numpy as jnp
import numpy as np
from jax import lax
from jax.experimental import pallas as pl
from jax.experimental.pallas import tpu as pltpu
from jax.sharding import PartitionSpec as P

ORDER = 3
LANES = 128
ROWS = 16
STAGGER_NS = 5500

f32 = jnp.float32
bf16 = jnp.bfloat16
highest = lax.Precision.HIGHEST


def phase_tables(seq_len):
    radix_len = math.gcd(seq_len, 128)
    outer_len = 2 * seq_len // radix_len
    half_outer = outer_len // 2
    total_len = 2 * seq_len
    low_index = jnp.arange(half_outer, dtype=jnp.int32)
    outer_index = jnp.arange(outer_len, dtype=jnp.int32)
    radix_index = jnp.arange(radix_len, dtype=jnp.int32)
    outer_angle = (low_index[:, None] * outer_index[None, :] % outer_len).astype(jnp.float32) * (
        2.0 * math.pi / outer_len
    )
    twist_angle = (outer_index[:, None] * radix_index[None, :] % total_len).astype(jnp.float32) * (
        2.0 * math.pi / total_len
    )
    radix_angle = (radix_index[:, None] * radix_index[None, :] % radix_len).astype(jnp.float32) * (
        2.0 * math.pi / radix_len
    )
    return (
        jnp.cos(outer_angle),
        jnp.sin(outer_angle),
        jnp.cos(twist_angle),
        jnp.sin(twist_angle),
        jnp.cos(radix_angle),
        jnp.sin(radix_angle),
    )


def forward_spectrum(signal, tables):
    outer_cos, outer_sin, twist_cos, twist_sin, radix_cos, radix_sin = tables
    channels = signal.shape[0]
    folded = signal.reshape(channels, outer_cos.shape[0], radix_cos.shape[0])
    first_real = jnp.einsum("chr,hk->ckr", folded, outer_cos, precision=highest)
    first_imag = -jnp.einsum("chr,hk->ckr", folded, outer_sin, precision=highest)
    turned_real = first_real * twist_cos + first_imag * twist_sin
    turned_imag = first_imag * twist_cos - first_real * twist_sin
    spec_real = jnp.einsum("ckr,rq->ckq", turned_real, radix_cos, precision=highest) + jnp.einsum(
        "ckr,rq->ckq", turned_imag, radix_sin, precision=highest
    )
    spec_imag = jnp.einsum("ckr,rq->ckq", turned_imag, radix_cos, precision=highest) - jnp.einsum(
        "ckr,rq->ckq", turned_real, radix_sin, precision=highest
    )
    return (spec_real, spec_imag)


def inverse_spectrum(spec_real, spec_imag, tables):
    outer_cos, outer_sin, twist_cos, twist_sin, radix_cos, radix_sin = tables
    back_real = jnp.einsum("ckq,rq->ckr", spec_real, radix_cos, precision=highest) - jnp.einsum(
        "ckq,rq->ckr", spec_imag, radix_sin, precision=highest
    )
    back_imag = jnp.einsum("ckq,rq->ckr", spec_real, radix_sin, precision=highest) + jnp.einsum(
        "ckq,rq->ckr", spec_imag, radix_cos, precision=highest
    )
    untwist_real = back_real * twist_cos - back_imag * twist_sin
    untwist_imag = back_real * twist_sin + back_imag * twist_cos
    folded = jnp.einsum("ckr,hk->chr", untwist_real, outer_cos, precision=highest) - jnp.einsum(
        "ckr,hk->chr", untwist_imag, outer_sin, precision=highest
    )
    channels = folded.shape[0]
    total_len = 2 * folded.shape[1] * folded.shape[2]
    return folded.reshape(channels, -1) / total_len


def local_general(inputs, cotangent, filters, mixing, ar_coef):
    tok_rows, local_width = inputs.shape
    ctx_count = lax.axis_size("ctx")
    ctx_place = lax.axis_index("ctx")
    narrow = local_width // ctx_count
    seq_len = tok_rows * ctx_count
    tables = phase_tables(seq_len)
    seq_cols = lax.all_to_all(inputs.T, "ctx", split_axis=0, concat_axis=1, tiled=True)
    signal = seq_cols.astype(jnp.float32)
    filter_all = lax.all_gather(filters, "ctx", axis=0, tiled=True)
    mix_local = lax.dynamic_slice_in_dim(mixing, ctx_place * narrow, narrow, 1)
    kernel = jnp.einsum("lk,kc->cl", filter_all, mix_local, precision=highest)
    sig_real, sig_imag = forward_spectrum(signal, tables)
    ker_real, ker_imag = forward_spectrum(kernel, tables)
    convolved = inverse_spectrum(
        ker_real * sig_real - ker_imag * sig_imag, ker_real * sig_imag + ker_imag * sig_real, tables
    )
    cot_cols = lax.all_to_all(cotangent.T, "ctx", split_axis=0, concat_axis=1, tiled=True)
    cot_real, cot_imag = forward_spectrum(cot_cols.astype(jnp.float32), tables)
    lagged = inverse_spectrum(
        cot_real * sig_real + cot_imag * sig_imag, cot_imag * sig_real - cot_real * sig_imag, tables
    )
    ar_local = lax.dynamic_slice_in_dim(ar_coef, ctx_place * narrow, narrow, 1)
    padded = jnp.pad(signal, ((0, 0), (ORDER, 0)))
    autoreg = jnp.zeros_like(signal)
    for lag_step in range(1, ORDER + 1):
        autoreg = (
            autoreg
            + ar_local[lag_step - 1][:, None]
            * padded[:, ORDER - lag_step : ORDER - lag_step + seq_len]
        )
    out_cols = (convolved + autoreg).astype(jnp.bfloat16)
    outputs = lax.all_to_all(out_cols, "ctx", split_axis=1, concat_axis=0, tiled=True).T
    mix_piece = jnp.einsum("lk,cl->kc", filter_all, lagged, precision=highest)
    grad_mixing, grad_ar = (
        lax.all_gather(mix_piece, "ctx", axis=1, tiled=True),
        lax.all_gather(lagged[:, 1 : ORDER + 1].T, "ctx", axis=1, tiled=True),
    )
    return (outputs, grad_mixing, grad_ar)


def split_pair(value):
    high = value.astype(bf16)
    return high, (value - high.astype(f32)).astype(bf16)


def turn(count, k):
    angle = math.pi * (k + 0.5) / count
    return math.cos(angle), math.sin(angle)


def half_forward(xs):
    n = len(xs)
    if n == 1:
        return [(xs[0], None)]
    even, odd = half_forward(xs[0::2]), half_forward(xs[1::2])
    low, high = [], []
    for k in range(n // 2):
        c, s = turn(n, k)
        er, ei = even[k]
        orr, oi = odd[k]
        if oi is None:
            tr, ti = orr * c, orr * (-s)
            low.append((er + tr, ti))
            high.append((er - tr, ti))
        else:
            tr, ti = orr * c + oi * s, oi * c - orr * s
            low.append((er + tr, ei + ti))
            high.append((er - tr, ti - ei))
    return low + high[::-1]


def half_inverse(us):
    n = len(us)
    if n == 1:
        return [us[0][0]]
    even, odd = [], []
    for k in range(n // 2):
        c, s = turn(n, k)
        (ar, ai), (br, bi) = us[k], us[n - 1 - k]
        dr, di = ar - br, ai + bi
        if n == 2:
            even.append((ar + br, None))
            odd.append((dr * c - di * s, None))
        else:
            even.append((ar + br, ai - bi))
            odd.append((dr * c - di * s, dr * s + di * c))
    out = [None] * n
    out[0::2] = half_inverse(even)
    out[1::2] = half_inverse(odd)
    return out


def dft_constants(half, radix):
    index = np.arange(radix)
    angle = 2.0 * np.pi * (index[:, None] * index[None, :] % radix) / radix
    c, s = np.cos(angle), np.sin(angle)
    forward = np.block([[c, s], [-s, c]])

    def stacked(matrix):
        matrix = matrix.astype(np.float32)
        high = matrix.astype(jnp.bfloat16)
        low = (matrix - high.astype(np.float32)).astype(jnp.bfloat16)
        return np.concatenate([high, low], axis=0)

    theta = 2.0 * np.pi * index[:, None] * (np.arange(half)[None, :] + 0.5) / (2 * half * radix)
    twist = np.concatenate([np.cos(theta), np.sin(theta)], axis=1).astype(np.float32)
    table = np.zeros((radix + 2 * half, radix), np.float32)
    table[:radix, : 2 * half] = twist
    table[radix:] = twist.T
    return stacked(forward), stacked(forward.T), table


def dot(a, b):
    return jnp.dot(a, b, preferred_element_type=f32)


def outer_forward(src_ref, start, tw_ref, high_ref, low_ref, half, radix, slot):
    for r in range(0, radix, ROWS):
        parts = half_forward([src_ref[slot[h], start + r : start + r + ROWS, :].astype(f32) for h in range(half)])
        for k, (re, im) in enumerate(parts):
            c, s = tw_ref[r : r + ROWS, k : k + 1], tw_ref[r : r + ROWS, half + k : half + k + 1]
            lanes = slice(k * LANES, (k + 1) * LANES)
            for base, value in ((0, re * c + im * s), (radix, im * c - re * s)):
                high, low = split_pair(value)
                high_ref[base + r : base + r + ROWS, lanes] = high
                low_ref[base + r : base + r + ROWS, lanes] = low


def inner_dft(w_ref, high_ref, low_ref, lanes):
    both = w_ref.shape[0] // 2
    first = dot(w_ref[...], high_ref[:, lanes])
    return first[:both] + first[both:] + dot(w_ref[:both, :], low_ref[:, lanes])


def pack_kernel(place_ref, x_ref, g_ref, f_ref, send_ref, fbuf, sems, *, wait, slot):
    count = send_ref.shape[0]
    tok = x_ref.shape[0]
    taps_in = pltpu.make_async_copy(f_ref, fbuf, sems.at[2 * count])
    taps_in.start()
    copies = []
    for j in range(count):
        lanes = pl.ds(j * LANES, LANES)
        for side, src in enumerate((x_ref, g_ref)):
            copy = pltpu.make_async_copy(
                src.at[:, lanes], send_ref.at[slot[j], pl.ds(side * tok, tok), :], sems.at[2 * j + side]
            )
            copy.start()
            copies.append(copy)

    @pl.when(lax.axis_index("mp") == 0)
    def _():
        pl.delay(wait)

    taps_in.wait()
    high, low = split_pair(fbuf[...])
    pieces = jnp.concatenate([high.astype(f32), low.astype(f32)], axis=0).astype(bf16)
    for j in range(count):
        send_ref[j, 2 * tok :, :] = pieces
    for copy in copies:
        copy.wait()


def main_kernel(
    place_ref,
    recv_ref,
    mix_ref,
    ar_ref,
    wf_ref,
    wi_ref,
    tw_ref,
    out_ref,
    a_high,
    a_low,
    b_high,
    b_low,
    spec_ref,
    taps_ref,
    p_high,
    p_low,
    *,
    half,
    radix,
    kp,
    slot,
):
    taps = mix_ref.shape[0]
    order = ar_ref.shape[0]
    width = 2 * radix
    scale = 1.0 / (half * radix)
    blocks = []
    for h in range(half):
        both = recv_ref[slot[h], 2 * radix : 2 * radix + 2 * taps, :].astype(f32)
        value = both[:taps] + both[taps:]
        extra = jnp.zeros((kp - taps, radix), f32)
        if h == 0:
            row = lax.broadcasted_iota(jnp.int32, extra.shape, 0)
            lane = lax.broadcasted_iota(jnp.int32, extra.shape, 1)
            extra = jnp.where((row < order) & (lane == row + 1), 1.0, extra)
        blocks.append(jnp.concatenate([value, extra], axis=0))
    for k, (re, im) in enumerate(half_forward(blocks)):
        c, s = tw_ref[radix + k : radix + k + 1, :], tw_ref[radix + half + k : radix + half + k + 1, :]
        value = jnp.concatenate([re * c + im * s, im * c - re * s], axis=1)
        high, low = split_pair(value)
        a_high[k * kp : (k + 1) * kp, 0:width] = high
        a_low[k * kp : (k + 1) * kp, 0:width] = low
    n_rows = half * kp
    filt = (
        dot(a_high[0:n_rows, 0:width], wi_ref[0:width, :])
        + dot(a_low[0:n_rows, 0:width], wi_ref[0:width, :])
        + dot(a_high[0:n_rows, 0:width], wi_ref[width : 2 * width, :])
    )
    f_high, f_low = split_pair(filt)
    for k in range(half):
        rows = slice(k * kp, (k + 1) * kp)
        lanes = slice(k * width, (k + 1) * width)
        taps_ref[0:kp, lanes] = f_high[rows]
        taps_ref[kp : 2 * kp, lanes] = f_low[rows]
    weights = (
        jnp.concatenate([mix_ref[...], ar_ref[...], jnp.zeros((kp - taps - order, LANES), f32)], axis=0)
        * scale
    )
    m_high, m_low = split_pair(weights)
    zero = jnp.zeros_like(m_high)

    def diagonal(m):
        return jnp.concatenate(
            [jnp.concatenate([m, zero], axis=1), jnp.concatenate([zero, m], axis=1)], axis=0
        )

    d_high, d_low = diagonal(m_high), diagonal(m_low)
    mixer = jnp.concatenate([d_high, d_high, d_low], axis=0)

    outer_forward(recv_ref, 0, tw_ref, b_high, b_low, half, radix, slot)
    for m in range(half // 2):
        lanes = slice(m * 2 * LANES, (m + 1) * 2 * LANES)
        rows = slice(2 * m * kp, 2 * (m + 1) * kp)
        spec = inner_dft(wf_ref, b_high, b_low, lanes)
        spec_ref[:, lanes] = spec
        ker = lax.dot_general(
            jnp.concatenate([f_high[rows], f_low[rows], f_high[rows]], axis=0),
            mixer,
            (((0,), (0,)), ((), ())),
            preferred_element_type=f32,
        )
        sr, si, kr, ki = spec[:radix], spec[radix:], ker[:radix], ker[radix:]
        for base, value in ((0, sr * kr - si * ki), (radix, sr * ki + si * kr)):
            high, low = split_pair(value)
            a_high[base : base + radix, lanes] = high
            a_low[base : base + radix, lanes] = low
    backs = []
    for m in range(half // 2):
        lanes = slice(m * 2 * LANES, (m + 1) * 2 * LANES)
        backs.append(inner_dft(wi_ref, a_high, a_low, lanes))
    for r in range(0, radix, ROWS):
        us = []
        for k in range(half):
            lanes = slice((k % 2) * LANES, (k % 2 + 1) * LANES)
            gr = backs[k // 2][r : r + ROWS, lanes]
            gi = backs[k // 2][radix + r : radix + r + ROWS, lanes]
            c, s = tw_ref[r : r + ROWS, k : k + 1], tw_ref[r : r + ROWS, half + k : half + k + 1]
            us.append((gr * c - gi * s, gr * s + gi * c))
        for h, value in enumerate(half_inverse(us)):
            out_ref[slot[h], r : r + ROWS, :] = value.astype(bf16)

    outer_forward(recv_ref, radix, tw_ref, b_high, b_low, half, radix, slot)
    for m in range(half // 2):
        lanes = slice(m * 2 * LANES, (m + 1) * 2 * LANES)
        cot = inner_dft(wf_ref, b_high, b_low, lanes)
        spec = spec_ref[:, lanes]
        cr, ci, sr, si = cot[:radix], cot[radix:], spec[:radix], spec[radix:]
        for base, value in ((0, cr * sr + ci * si), (radix, ci * sr - cr * si)):
            high, low = split_pair(value)
            for side in range(2):
                row = (2 * m + side) * 2 * radix + base
                part = slice(side * LANES, (side + 1) * LANES)
                p_high[row : row + radix, :] = high[:, part]
                p_low[row : row + radix, :] = low[:, part]
    first = dot(taps_ref[...], p_high[...])
    grads = (first[:kp] + first[kp:] + dot(taps_ref[0:kp, :], p_low[...])) * scale
    g_high, g_low = split_pair(grads)
    used = taps + order
    fill = out_ref.shape[1] - radix - 2 * used
    pieces = [g_high.astype(f32)[:used], g_low.astype(f32)[:used]]
    if fill:
        pieces.append(jnp.zeros((fill, LANES), f32))
    pieces = jnp.concatenate(pieces, axis=0).astype(bf16)
    for j in range(out_ref.shape[0]):
        out_ref[j, radix:, :] = pieces


def unpack_kernel(back_ref, out_ref, mix_ref, ar_ref, mix_buf, ar_buf, sems, *, slot):
    count = back_ref.shape[0]
    tok = out_ref.shape[0]
    taps, order = mix_ref.shape[0], ar_ref.shape[0]
    used = taps + order
    copies = []
    for j in range(count):
        lanes = pl.ds(j * LANES, LANES)
        copy = pltpu.make_async_copy(back_ref.at[slot[j], pl.ds(0, tok), :], out_ref.at[:, lanes], sems.at[j])
        copy.start()
        copies.append(copy)
    for j in range(count):
        lanes = slice(j * LANES, (j + 1) * LANES)
        pieces = back_ref[slot[j], tok:, :].astype(f32)
        grads = pieces[0:used] + pieces[used : 2 * used]
        mix_buf[:, lanes] = grads[0:taps]
        ar_buf[:, lanes] = grads[taps:used]
    for buf, ref, place in ((mix_buf, mix_ref, count), (ar_buf, ar_ref, count + 1)):
        copy = pltpu.make_async_copy(buf, ref, sems.at[place])
        copy.start()
        copies.append(copy)
    for copy in copies:
        copy.wait()


def shape_of(*dims, dtype=f32):
    return jax.ShapeDtypeStruct(dims, dtype)


def local_tiled(inputs, cotangent, filters, mixing, ar_coef):
    tok_rows, local_width = inputs.shape
    count = lax.axis_size("ctx")
    taps, order = filters.shape[1], ar_coef.shape[0]
    half, radix = count, tok_rows
    kp = -(-(taps + order) // 8) * 8
    wf, wi, twist = dft_constants(half, radix)
    rows = 2 * tok_rows + 2 * taps
    back_rows = -(-(tok_rows + 2 * (taps + order)) // 8) * 8
    ranks = list(range(count))[::-1]
    slot = [ranks.index(i) for i in range(count)]
    swap = functools.partial(
        lax.all_to_all,
        axis_name="ctx",
        split_axis=0,
        concat_axis=0,
        tiled=True,
        axis_index_groups=[ranks],
    )
    small = pltpu.CompilerParams(vmem_limit_bytes=8 << 20)

    place = lax.axis_index("ctx").astype(jnp.int32).reshape(1)
    stay = functools.partial(pltpu.with_memory_space_constraint, memory_space=pltpu.HBM)
    send = pl.pallas_call(
        functools.partial(pack_kernel, wait=STAGGER_NS, slot=slot),
        out_shape=shape_of(count, rows, LANES, dtype=bf16),
        in_specs=[pl.BlockSpec(memory_space=pltpu.SMEM)] + [pl.BlockSpec(memory_space=pltpu.HBM)] * 3,
        out_specs=pl.BlockSpec(memory_space=pltpu.VMEM),
        scratch_shapes=[
            pltpu.VMEM((taps, tok_rows), f32),
            pltpu.SemaphoreType.DMA((2 * count + 1,)),
        ],
        compiler_params=small,
        name="pack",
    )(place, stay(inputs), stay(cotangent), stay(filters.T))
    recv = swap(send)

    whole = lambda *dims: pl.BlockSpec(dims, lambda i, place: (0,) * len(dims))
    span = half * LANES
    split = pltpu.VMEM((2 * radix, span), bf16)
    tall = pltpu.VMEM((half * 2 * radix, LANES), bf16)
    result = pl.pallas_call(
        functools.partial(main_kernel, half=half, radix=radix, kp=kp, slot=slot),
        out_shape=shape_of(count, back_rows, LANES, dtype=bf16),
        grid_spec=pltpu.PrefetchScalarGridSpec(
            num_scalar_prefetch=1,
            grid=(1,),
            in_specs=[
                whole(count, rows, LANES),
                pl.BlockSpec((taps, LANES), lambda i, place: (0, place[0])),
                pl.BlockSpec((order, LANES), lambda i, place: (0, place[0])),
                whole(*wf.shape),
                whole(*wi.shape),
                whole(*twist.shape),
            ],
            out_specs=whole(count, back_rows, LANES),
            scratch_shapes=[split] * 4
            + [pltpu.VMEM((2 * radix, span), f32), pltpu.VMEM((2 * kp, half * 2 * radix), bf16)]
            + [tall] * 2,
        ),
        compiler_params=pltpu.CompilerParams(vmem_limit_bytes=24 << 20),
        name="main",
    )(place, recv, mixing, ar_coef, wf, wi, twist)
    back = swap(result)

    return pl.pallas_call(
        functools.partial(unpack_kernel, slot=slot),
        out_shape=(
            shape_of(tok_rows, local_width, dtype=bf16),
            shape_of(taps, local_width),
            shape_of(order, local_width),
        ),
        in_specs=[pl.BlockSpec(memory_space=pltpu.VMEM)],
        out_specs=[pl.BlockSpec(memory_space=pl.ANY)] * 3,
        scratch_shapes=[
            pltpu.VMEM((taps, local_width), f32),
            pltpu.VMEM((order, local_width), f32),
            pltpu.SemaphoreType.DMA((count + 2,)),
        ],
        compiler_params=small,
        name="unpack",
    )(back)


def local(inputs, cotangent, filters, mixing, ar_coef):
    tok_rows, local_width = inputs.shape
    count = lax.axis_size("ctx")
    tiled = (
        local_width == count * LANES
        and tok_rows == LANES
        and count in (2, 4, 8)
        and filters.shape[1] % 8 == 0
    )
    return (local_tiled if tiled else local_general)(inputs, cotangent, filters, mixing, ar_coef)


def solution(mesh):
    return jax.shard_map(
        local,
        mesh=mesh,
        in_specs=(
            P(("groups", "ctx"), "mp"),
            P(("groups", "ctx"), "mp"),
            P("ctx", None),
            P(None, "mp"),
            P(None, "mp"),
        ),
        out_specs=(P(("groups", "ctx"), "mp"), P("groups", "mp"), P("groups", "mp")),
        check_vma=False,
    )
```

```python
import functools
import math

import jax
import jax.numpy as jnp
import numpy as np
from jax import lax
from jax.experimental import pallas as pl
from jax.experimental.pallas import tpu as pltpu
from jax.sharding import PartitionSpec as P

ORDER = 3
LANES = 128
ROWS = 16
STAGGER_NS = 5500

f32 = jnp.float32
bf16 = jnp.bfloat16
highest = lax.Precision.HIGHEST


def phase_tables(seq_len):
    radix_len = math.gcd(seq_len, 128)
    outer_len = 2 * seq_len // radix_len
    half_outer = outer_len // 2
    total_len = 2 * seq_len
    low_index = jnp.arange(half_outer, dtype=jnp.int32)
    outer_index = jnp.arange(outer_len, dtype=jnp.int32)
    radix_index = jnp.arange(radix_len, dtype=jnp.int32)
    outer_angle = (low_index[:, None] * outer_index[None, :] % outer_len).astype(jnp.float32) * (
        2.0 * math.pi / outer_len
    )
    twist_angle = (outer_index[:, None] * radix_index[None, :] % total_len).astype(jnp.float32) * (
        2.0 * math.pi / total_len
    )
    radix_angle = (radix_index[:, None] * radix_index[None, :] % radix_len).astype(jnp.float32) * (
        2.0 * math.pi / radix_len
    )
    return (
        jnp.cos(outer_angle),
        jnp.sin(outer_angle),
        jnp.cos(twist_angle),
        jnp.sin(twist_angle),
        jnp.cos(radix_angle),
        jnp.sin(radix_angle),
    )


def forward_spectrum(signal, tables):
    outer_cos, outer_sin, twist_cos, twist_sin, radix_cos, radix_sin = tables
    channels = signal.shape[0]
    folded = signal.reshape(channels, outer_cos.shape[0], radix_cos.shape[0])
    first_real = jnp.einsum("chr,hk->ckr", folded, outer_cos, precision=highest)
    first_imag = -jnp.einsum("chr,hk->ckr", folded, outer_sin, precision=highest)
    turned_real = first_real * twist_cos + first_imag * twist_sin
    turned_imag = first_imag * twist_cos - first_real * twist_sin
    spec_real = jnp.einsum("ckr,rq->ckq", turned_real, radix_cos, precision=highest) + jnp.einsum(
        "ckr,rq->ckq", turned_imag, radix_sin, precision=highest
    )
    spec_imag = jnp.einsum("ckr,rq->ckq", turned_imag, radix_cos, precision=highest) - jnp.einsum(
        "ckr,rq->ckq", turned_real, radix_sin, precision=highest
    )
    return (spec_real, spec_imag)


def inverse_spectrum(spec_real, spec_imag, tables):
    outer_cos, outer_sin, twist_cos, twist_sin, radix_cos, radix_sin = tables
    back_real = jnp.einsum("ckq,rq->ckr", spec_real, radix_cos, precision=highest) - jnp.einsum(
        "ckq,rq->ckr", spec_imag, radix_sin, precision=highest
    )
    back_imag = jnp.einsum("ckq,rq->ckr", spec_real, radix_sin, precision=highest) + jnp.einsum(
        "ckq,rq->ckr", spec_imag, radix_cos, precision=highest
    )
    untwist_real = back_real * twist_cos - back_imag * twist_sin
    untwist_imag = back_real * twist_sin + back_imag * twist_cos
    folded = jnp.einsum("ckr,hk->chr", untwist_real, outer_cos, precision=highest) - jnp.einsum(
        "ckr,hk->chr", untwist_imag, outer_sin, precision=highest
    )
    channels = folded.shape[0]
    total_len = 2 * folded.shape[1] * folded.shape[2]
    return folded.reshape(channels, -1) / total_len


def local_general(inputs, cotangent, filters, mixing, ar_coef):
    tok_rows, local_width = inputs.shape
    ctx_count = lax.axis_size("ctx")
    ctx_place = lax.axis_index("ctx")
    narrow = local_width // ctx_count
    seq_len = tok_rows * ctx_count
    tables = phase_tables(seq_len)
    seq_cols = lax.all_to_all(inputs.T, "ctx", split_axis=0, concat_axis=1, tiled=True)
    signal = seq_cols.astype(jnp.float32)
    filter_all = lax.all_gather(filters, "ctx", axis=0, tiled=True)
    mix_local = lax.dynamic_slice_in_dim(mixing, ctx_place * narrow, narrow, 1)
    kernel = jnp.einsum("lk,kc->cl", filter_all, mix_local, precision=highest)
    sig_real, sig_imag = forward_spectrum(signal, tables)
    ker_real, ker_imag = forward_spectrum(kernel, tables)
    convolved = inverse_spectrum(
        ker_real * sig_real - ker_imag * sig_imag, ker_real * sig_imag + ker_imag * sig_real, tables
    )
    cot_cols = lax.all_to_all(cotangent.T, "ctx", split_axis=0, concat_axis=1, tiled=True)
    cot_real, cot_imag = forward_spectrum(cot_cols.astype(jnp.float32), tables)
    lagged = inverse_spectrum(
        cot_real * sig_real + cot_imag * sig_imag, cot_imag * sig_real - cot_real * sig_imag, tables
    )
    ar_local = lax.dynamic_slice_in_dim(ar_coef, ctx_place * narrow, narrow, 1)
    padded = jnp.pad(signal, ((0, 0), (ORDER, 0)))
    autoreg = jnp.zeros_like(signal)
    for lag_step in range(1, ORDER + 1):
        autoreg = (
            autoreg
            + ar_local[lag_step - 1][:, None]
            * padded[:, ORDER - lag_step : ORDER - lag_step + seq_len]
        )
    out_cols = (convolved + autoreg).astype(jnp.bfloat16)
    outputs = lax.all_to_all(out_cols, "ctx", split_axis=1, concat_axis=0, tiled=True).T
    mix_piece = jnp.einsum("lk,cl->kc", filter_all, lagged, precision=highest)
    grad_mixing, grad_ar = (
        lax.all_gather(mix_piece, "ctx", axis=1, tiled=True),
        lax.all_gather(lagged[:, 1 : ORDER + 1].T, "ctx", axis=1, tiled=True),
    )
    return (outputs, grad_mixing, grad_ar)


def split_pair(value):
    high = value.astype(bf16)
    return high, (value - high.astype(f32)).astype(bf16)


def turn(count, k):
    angle = math.pi * (k + 0.5) / count
    return math.cos(angle), math.sin(angle)


def half_forward(xs):
    n = len(xs)
    if n == 1:
        return [(xs[0], None)]
    even, odd = half_forward(xs[0::2]), half_forward(xs[1::2])
    low, high = [], []
    for k in range(n // 2):
        c, s = turn(n, k)
        er, ei = even[k]
        orr, oi = odd[k]
        if oi is None:
            tr, ti = orr * c, orr * (-s)
            low.append((er + tr, ti))
            high.append((er - tr, ti))
        else:
            tr, ti = orr * c + oi * s, oi * c - orr * s
            low.append((er + tr, ei + ti))
            high.append((er - tr, ti - ei))
    return low + high[::-1]


def half_inverse(us):
    n = len(us)
    if n == 1:
        return [us[0][0]]
    even, odd = [], []
    for k in range(n // 2):
        c, s = turn(n, k)
        (ar, ai), (br, bi) = us[k], us[n - 1 - k]
        dr, di = ar - br, ai + bi
        if n == 2:
            even.append((ar + br, None))
            odd.append((dr * c - di * s, None))
        else:
            even.append((ar + br, ai - bi))
            odd.append((dr * c - di * s, dr * s + di * c))
    out = [None] * n
    out[0::2] = half_inverse(even)
    out[1::2] = half_inverse(odd)
    return out


def dft_constants(half, radix):
    index = np.arange(radix)
    angle = 2.0 * np.pi * (index[:, None] * index[None, :] % radix) / radix
    c, s = np.cos(angle), np.sin(angle)
    forward = np.block([[c, s], [-s, c]])

    def stacked(matrix):
        matrix = matrix.astype(np.float32)
        high = matrix.astype(jnp.bfloat16)
        low = (matrix - high.astype(np.float32)).astype(jnp.bfloat16)
        return np.concatenate([high, low], axis=0)

    theta = 2.0 * np.pi * index[:, None] * (np.arange(half)[None, :] + 0.5) / (2 * half * radix)
    twist = np.concatenate([np.cos(theta), np.sin(theta)], axis=1).astype(np.float32)
    table = np.zeros((radix + 2 * half, radix), np.float32)
    table[:radix, : 2 * half] = twist
    table[radix:] = twist.T
    return stacked(forward), stacked(forward.T), table


def dot(a, b):
    return jnp.dot(a, b, preferred_element_type=f32)


def outer_forward(src_ref, start, tw_ref, high_ref, low_ref, half, radix, slot):
    for r in range(0, radix, ROWS):
        parts = half_forward([src_ref[slot[h], start + r : start + r + ROWS, :].astype(f32) for h in range(half)])
        for k, (re, im) in enumerate(parts):
            c, s = tw_ref[r : r + ROWS, k : k + 1], tw_ref[r : r + ROWS, half + k : half + k + 1]
            lanes = slice(k * LANES, (k + 1) * LANES)
            for base, value in ((0, re * c + im * s), (radix, im * c - re * s)):
                high, low = split_pair(value)
                high_ref[base + r : base + r + ROWS, lanes] = high
                low_ref[base + r : base + r + ROWS, lanes] = low


def inner_dft(w_ref, high_ref, low_ref, lanes):
    both = w_ref.shape[0] // 2
    first = dot(w_ref[...], high_ref[:, lanes])
    return first[:both] + first[both:] + dot(w_ref[:both, :], low_ref[:, lanes])


def pack_kernel(place_ref, x_ref, g_ref, f_ref, send_ref, fbuf, sems, *, wait, slot):
    count = send_ref.shape[0]
    tok = x_ref.shape[0]
    taps_in = pltpu.make_async_copy(f_ref, fbuf, sems.at[2 * count])
    taps_in.start()
    copies = []
    for j in range(count):
        lanes = pl.ds(j * LANES, LANES)
        for side, src in enumerate((x_ref, g_ref)):
            copy = pltpu.make_async_copy(
                src.at[:, lanes], send_ref.at[slot[j], pl.ds(side * tok, tok), :], sems.at[2 * j + side]
            )
            copy.start()
            copies.append(copy)

    @pl.when(lax.axis_index("mp") == 0)
    def _():
        pl.delay(wait)

    taps_in.wait()
    high, low = split_pair(fbuf[...])
    pieces = jnp.concatenate([high.astype(f32), low.astype(f32)], axis=0).astype(bf16)
    for j in range(count):
        send_ref[j, 2 * tok :, :] = pieces
    for copy in copies:
        copy.wait()


def main_kernel(
    place_ref,
    recv_ref,
    mix_ref,
    ar_ref,
    wf_ref,
    wi_ref,
    tw_ref,
    out_ref,
    a_high,
    a_low,
    b_high,
    b_low,
    spec_ref,
    taps_ref,
    p_high,
    p_low,
    *,
    half,
    radix,
    kp,
    slot,
):
    taps = mix_ref.shape[0]
    order = ar_ref.shape[0]
    width = 2 * radix
    scale = 1.0 / (half * radix)
    blocks = []
    for h in range(half):
        both = recv_ref[slot[h], 2 * radix : 2 * radix + 2 * taps, :].astype(f32)
        value = both[:taps] + both[taps:]
        extra = jnp.zeros((kp - taps, radix), f32)
        if h == 0:
            row = lax.broadcasted_iota(jnp.int32, extra.shape, 0)
            lane = lax.broadcasted_iota(jnp.int32, extra.shape, 1)
            extra = jnp.where((row < order) & (lane == row + 1), 1.0, extra)
        blocks.append(jnp.concatenate([value, extra], axis=0))
    for k, (re, im) in enumerate(half_forward(blocks)):
        c, s = tw_ref[radix + k : radix + k + 1, :], tw_ref[radix + half + k : radix + half + k + 1, :]
        value = jnp.concatenate([re * c + im * s, im * c - re * s], axis=1)
        high, low = split_pair(value)
        a_high[k * kp : (k + 1) * kp, 0:width] = high
        a_low[k * kp : (k + 1) * kp, 0:width] = low
    n_rows = half * kp
    filt = (
        dot(a_high[0:n_rows, 0:width], wi_ref[0:width, :])
        + dot(a_low[0:n_rows, 0:width], wi_ref[0:width, :])
        + dot(a_high[0:n_rows, 0:width], wi_ref[width : 2 * width, :])
    )
    f_high, f_low = split_pair(filt)
    for k in range(half):
        rows = slice(k * kp, (k + 1) * kp)
        lanes = slice(k * width, (k + 1) * width)
        taps_ref[0:kp, lanes] = f_high[rows]
        taps_ref[kp : 2 * kp, lanes] = f_low[rows]
    weights = (
        jnp.concatenate([mix_ref[...], ar_ref[...], jnp.zeros((kp - taps - order, LANES), f32)], axis=0)
        * scale
    )
    m_high, m_low = split_pair(weights)
    zero = jnp.zeros_like(m_high)

    def diagonal(m):
        return jnp.concatenate(
            [jnp.concatenate([m, zero], axis=1), jnp.concatenate([zero, m], axis=1)], axis=0
        )

    d_high, d_low = diagonal(m_high), diagonal(m_low)
    mixer = jnp.concatenate([d_high, d_high, d_low], axis=0)

    outer_forward(recv_ref, 0, tw_ref, b_high, b_low, half, radix, slot)
    for m in range(half // 2):
        lanes = slice(m * 2 * LANES, (m + 1) * 2 * LANES)
        rows = slice(2 * m * kp, 2 * (m + 1) * kp)
        spec = inner_dft(wf_ref, b_high, b_low, lanes)
        spec_ref[:, lanes] = spec
        ker = lax.dot_general(
            jnp.concatenate([f_high[rows], f_low[rows], f_high[rows]], axis=0),
            mixer,
            (((0,), (0,)), ((), ())),
            preferred_element_type=f32,
        )
        sr, si, kr, ki = spec[:radix], spec[radix:], ker[:radix], ker[radix:]
        for base, value in ((0, sr * kr - si * ki), (radix, sr * ki + si * kr)):
            high, low = split_pair(value)
            a_high[base : base + radix, lanes] = high
            a_low[base : base + radix, lanes] = low
    backs = []
    for m in range(half // 2):
        lanes = slice(m * 2 * LANES, (m + 1) * 2 * LANES)
        backs.append(inner_dft(wi_ref, a_high, a_low, lanes))
    for r in range(0, radix, ROWS):
        us = []
        for k in range(half):
            lanes = slice((k % 2) * LANES, (k % 2 + 1) * LANES)
            gr = backs[k // 2][r : r + ROWS, lanes]
            gi = backs[k // 2][radix + r : radix + r + ROWS, lanes]
            c, s = tw_ref[r : r + ROWS, k : k + 1], tw_ref[r : r + ROWS, half + k : half + k + 1]
            us.append((gr * c - gi * s, gr * s + gi * c))
        for h, value in enumerate(half_inverse(us)):
            out_ref[slot[h], r : r + ROWS, :] = value.astype(bf16)

    outer_forward(recv_ref, radix, tw_ref, b_high, b_low, half, radix, slot)
    for m in range(half // 2):
        lanes = slice(m * 2 * LANES, (m + 1) * 2 * LANES)
        cot = inner_dft(wf_ref, b_high, b_low, lanes)
        spec = spec_ref[:, lanes]
        cr, ci, sr, si = cot[:radix], cot[radix:], spec[:radix], spec[radix:]
        for base, value in ((0, cr * sr + ci * si), (radix, ci * sr - cr * si)):
            high, low = split_pair(value)
            for side in range(2):
                row = (2 * m + side) * 2 * radix + base
                part = slice(side * LANES, (side + 1) * LANES)
                p_high[row : row + radix, :] = high[:, part]
                p_low[row : row + radix, :] = low[:, part]
    first = dot(taps_ref[...], p_high[...])
    grads = (first[:kp] + first[kp:] + dot(taps_ref[0:kp, :], p_low[...])) * scale
    g_high, g_low = split_pair(grads)
    used = taps + order
    fill = out_ref.shape[1] - radix - 2 * used
    pieces = [g_high.astype(f32)[:used], g_low.astype(f32)[:used]]
    if fill:
        pieces.append(jnp.zeros((fill, LANES), f32))
    pieces = jnp.concatenate(pieces, axis=0).astype(bf16)
    for j in range(out_ref.shape[0]):
        out_ref[j, radix:, :] = pieces


def unpack_kernel(back_ref, out_ref, mix_ref, ar_ref, mix_buf, ar_buf, sems, *, slot):
    count = back_ref.shape[0]
    tok = out_ref.shape[0]
    taps, order = mix_ref.shape[0], ar_ref.shape[0]
    used = taps + order
    copies = []
    for j in range(count):
        lanes = pl.ds(j * LANES, LANES)
        copy = pltpu.make_async_copy(back_ref.at[slot[j], pl.ds(0, tok), :], out_ref.at[:, lanes], sems.at[j])
        copy.start()
        copies.append(copy)
    for j in range(count):
        lanes = slice(j * LANES, (j + 1) * LANES)
        pieces = back_ref[slot[j], tok:, :].astype(f32)
        grads = pieces[0:used] + pieces[used : 2 * used]
        mix_buf[:, lanes] = grads[0:taps]
        ar_buf[:, lanes] = grads[taps:used]
    for buf, ref, place in ((mix_buf, mix_ref, count), (ar_buf, ar_ref, count + 1)):
        copy = pltpu.make_async_copy(buf, ref, sems.at[place])
        copy.start()
        copies.append(copy)
    for copy in copies:
        copy.wait()


def shape_of(*dims, dtype=f32):
    return jax.ShapeDtypeStruct(dims, dtype)


def local_tiled(inputs, cotangent, filters, mixing, ar_coef):
    tok_rows, local_width = inputs.shape
    count = lax.axis_size("ctx")
    taps, order = filters.shape[1], ar_coef.shape[0]
    half, radix = count, tok_rows
    kp = -(-(taps + order) // 8) * 8
    wf, wi, twist = dft_constants(half, radix)
    rows = 2 * tok_rows + 2 * taps
    back_rows = -(-(tok_rows + 2 * (taps + order)) // 8) * 8
    ranks = [i ^ (i >> 1) for i in range(count)][::-1]
    slot = [ranks.index(i) for i in range(count)]
    swap = functools.partial(
        lax.all_to_all,
        axis_name="ctx",
        split_axis=0,
        concat_axis=0,
        tiled=True,
        axis_index_groups=[ranks],
    )
    small = pltpu.CompilerParams(vmem_limit_bytes=8 << 20)

    place = lax.axis_index("ctx").astype(jnp.int32).reshape(1)
    stay = functools.partial(pltpu.with_memory_space_constraint, memory_space=pltpu.HBM)
    send = pl.pallas_call(
        functools.partial(pack_kernel, wait=STAGGER_NS, slot=slot),
        out_shape=shape_of(count, rows, LANES, dtype=bf16),
        in_specs=[pl.BlockSpec(memory_space=pltpu.SMEM)] + [pl.BlockSpec(memory_space=pltpu.HBM)] * 3,
        out_specs=pl.BlockSpec(memory_space=pltpu.VMEM),
        scratch_shapes=[
            pltpu.VMEM((taps, tok_rows), f32),
            pltpu.SemaphoreType.DMA((2 * count + 1,)),
        ],
        compiler_params=small,
        name="pack",
    )(place, stay(inputs), stay(cotangent), stay(filters.T))
    recv = swap(send)

    whole = lambda *dims: pl.BlockSpec(dims, lambda i, place: (0,) * len(dims))
    span = half * LANES
    split = pltpu.VMEM((2 * radix, span), bf16)
    tall = pltpu.VMEM((half * 2 * radix, LANES), bf16)
    result = pl.pallas_call(
        functools.partial(main_kernel, half=half, radix=radix, kp=kp, slot=slot),
        out_shape=shape_of(count, back_rows, LANES, dtype=bf16),
        grid_spec=pltpu.PrefetchScalarGridSpec(
            num_scalar_prefetch=1,
            grid=(1,),
            in_specs=[
                whole(count, rows, LANES),
                pl.BlockSpec((taps, LANES), lambda i, place: (0, place[0])),
                pl.BlockSpec((order, LANES), lambda i, place: (0, place[0])),
                whole(*wf.shape),
                whole(*wi.shape),
                whole(*twist.shape),
            ],
            out_specs=whole(count, back_rows, LANES),
            scratch_shapes=[split] * 4
            + [pltpu.VMEM((2 * radix, span), f32), pltpu.VMEM((2 * kp, half * 2 * radix), bf16)]
            + [tall] * 2,
        ),
        compiler_params=pltpu.CompilerParams(vmem_limit_bytes=24 << 20),
        name="main",
    )(place, recv, mixing, ar_coef, wf, wi, twist)
    back = swap(result)

    return pl.pallas_call(
        functools.partial(unpack_kernel, slot=slot),
        out_shape=(
            shape_of(tok_rows, local_width, dtype=bf16),
            shape_of(taps, local_width),
            shape_of(order, local_width),
        ),
        in_specs=[pl.BlockSpec(memory_space=pltpu.VMEM)],
        out_specs=[pl.BlockSpec(memory_space=pl.ANY)] * 3,
        scratch_shapes=[
            pltpu.VMEM((taps, local_width), f32),
            pltpu.VMEM((order, local_width), f32),
            pltpu.SemaphoreType.DMA((count + 2,)),
        ],
        compiler_params=small,
        name="unpack",
    )(back)


def local(inputs, cotangent, filters, mixing, ar_coef):
    tok_rows, local_width = inputs.shape
    count = lax.axis_size("ctx")
    tiled = (
        local_width == count * LANES
        and tok_rows == LANES
        and count in (2, 4, 8)
        and filters.shape[1] % 8 == 0
    )
    return (local_tiled if tiled else local_general)(inputs, cotangent, filters, mixing, ar_coef)


def solution(mesh):
    return jax.shard_map(
        local,
        mesh=mesh,
        in_specs=(
            P(("groups", "ctx"), "mp"),
            P(("groups", "ctx"), "mp"),
            P("ctx", None),
            P(None, "mp"),
            P(None, "mp"),
        ),
        out_specs=(P(("groups", "ctx"), "mp"), P("groups", "mp"), P("groups", "mp")),
        check_vma=False,
    )
```
